32 devices in a mesh: row: 16 (over z, y, x), col: 2 (over core).
Axes of the slice: x: 2, y: 2, z: 4, core: 2. Of those that a mesh axis runs over, the one named last changes fastest.
Arguments:
- latent: bfloat16 [6144, 512], P('row', 'col'), may hold values from -6 to 6
- w_kv: bfloat16 [512, 8192], P('row', 'col'), may hold values from -0.25 to 0.25
- queries: bfloat16 [6144, 4096], P('row', 'col'), may hold values from -240 to 240
- w_out: bfloat16 [4096, 7168], P('row', 'col'), may hold values from -0.09375 to 0.09375
Outputs:
- mixed: bfloat16 [6144, 7168], P('row', 'col')
The draws below stay inside these ranges and needn't reach their ends.
All inputs are finite; a program needn't handle non-finite values.
Results may differ from the reference program's by a relative error of at most 0.012.
The reference program's roundings to bfloat16 on the way (of `key_values`, `weights` and `attended`) count: a program that leaves them out, or rounds other values in their place, can miss the bound.
Values may be sent and summed in bfloat16 or wider, within the bound.
No kernel may reach another device: no remote copies, remote signals or barrier semaphores. Data moves between devices by JAX's collectives and lax.ppermute only.
A program may use at most 128 MiB of HBM per device.

```python
import math
import jax
import jax.numpy as jnp
from jax import lax

D = 7168
HEADS = 32
HEAD = 128
LATENT = 512
TOKENS = 6144


def draw_queries(key, part):
    first = jax.random.fold_in(jax.random.fold_in(key, 17), 0)
    values = jnp.clip(jax.random.normal(first, (TOKENS, HEADS * HEAD), jnp.float32), -4.0, 4.0)
    return values.astype(jnp.bfloat16)


def shard_levels(key, extent, pieces, smallest, top_value):
    def one(dim, blocks):
        draws = jax.random.uniform(jax.random.fold_in(jax.random.fold_in(key, 6), dim), (blocks,), jnp.float32, smallest / len(pieces), top_value / len(pieces))
        return jnp.repeat(jnp.exp(draws), extent[dim] // blocks).reshape((-1,) + (1,) * (len(extent) - dim - 1))

    factor_of = one(*pieces[0])
    for cut in pieces[1:]:
        factor_of = factor_of * one(*cut)
    return factor_of


def gaussian(own_key, extent, scale, limit, shards=(), held_as=jnp.bfloat16):
    result = jax.random.normal(own_key, extent, jnp.float32) * scale
    if len(shards) > 0:
        result = shard_levels(own_key, extent, shards, -0.22, 0.18) * result
    return jnp.clip(result, min=-limit, max=limit).astype(held_as)


def setup_inputs(seed: int = 0) -> dict:
    seeds = jax.random.split(jax.random.key(seed), 5)
    latent = gaussian(seeds[0], (TOKENS, LATENT), 1.0, 6.0, ((0, 16), (1, 2)))
    w_kv = gaussian(seeds[1], (LATENT, 2 * HEADS * HEAD), LATENT ** -0.5, 0.25, ((0, 16), (1, 2)))
    queries = draw_queries(jax.random.fold_in(seeds[4], 71), 0)
    w_out = gaussian(seeds[3], (HEADS * HEAD, D), (HEADS * HEAD) ** -0.5, 0.09375, ((0, 16), (1, 2)))
    return {"latent": latent, "w_kv": w_kv, "queries": queries, "w_out": w_out}


NEG_FILL = -1e30


def reference(latent, w_kv, queries, w_out):
    key_values = jnp.dot(latent, w_kv, preferred_element_type=jnp.float32).astype(jnp.bfloat16)
    key_values = key_values.reshape(TOKENS, HEADS, 2 * HEAD).transpose(1, 0, 2)
    head_queries = queries.reshape(TOKENS, HEADS, HEAD).transpose(1, 0, 2)
    block_rows = math.gcd(TOKENS, 1024)
    score_scale = HEAD ** -0.5
    key_pos = jnp.arange(TOKENS, dtype=jnp.int32)

    def one_head(operands):
        query_head, pairs = operands
        keys_only = pairs[:, :HEAD]
        values_only = pairs[:, HEAD:]

        def one_block(first_row):
            query_block = lax.dynamic_slice_in_dim(query_head, first_row, block_rows, 0)
            scores = lax.dot_general(query_block, keys_only, (((1,), (1,)), ((), ())), preferred_element_type=jnp.float32) * score_scale
            query_pos = first_row + jnp.arange(block_rows, dtype=jnp.int32)
            allowed = key_pos[None, :] <= query_pos[:, None]
            scores = jnp.where(allowed, scores, NEG_FILL)
            highest = jnp.max(scores, axis=1, keepdims=True)
            weights = jnp.where(allowed, jnp.exp(scores - highest), 0.0)
            totals = jnp.sum(weights, axis=1, keepdims=True)
            summed = jnp.dot(weights.astype(jnp.bfloat16), values_only, preferred_element_type=jnp.float32)
            return (summed / totals).astype(jnp.bfloat16)

        starts = jnp.arange(TOKENS // block_rows, dtype=jnp.int32) * block_rows
        return lax.map(one_block, starts).reshape(TOKENS, HEAD)

    attended = lax.map(one_head, (head_queries, key_values))
    attended = attended.transpose(1, 0, 2).reshape(TOKENS, HEADS * HEAD)
    return jnp.dot(attended, w_out, preferred_element_type=jnp.float32).astype(jnp.bfloat16)
```

```python
import functools
import math

import jax
import jax.numpy as jnp
from jax import lax
from jax.experimental import pallas as pl
from jax.experimental.pallas import tpu as pltpu
from jax.sharding import Mesh, PartitionSpec as P

HEAD = 128
NEG_FILL = -1e30
VMEM_LIMIT = 56 * 1024 * 1024


def attention_kernel(place, q_ref, *refs, cols, tok, group, span, rate, parts):
    latents, (w_ref, o_ref, kv_sc, m_sc, acc_sc) = refs[:cols], refs[cols:]
    grp, mem = place[0], place[1]
    plane = tok * group
    total = kv_sc.shape[0]
    planes = total // plane
    block = pl.program_id(1)
    rows = tok // parts

    @pl.when(block == 0)
    def _():
        def expand(t, _):
            at = pl.ds(pl.multiple_of(t * plane, plane), plane)
            out = jnp.dot(latents[0][at, :], w_ref[0], preferred_element_type=jnp.float32)
            for s in range(1, cols):
                out += jnp.dot(latents[s][at, :], w_ref[s], preferred_element_type=jnp.float32)
            kv_sc[at, :] = out.astype(kv_sc.dtype)
            return 0

        lax.fori_loop(planes - 1 - grp, planes, expand, 0)

    m_sc[...] = jnp.full_like(m_sc, NEG_FILL)
    acc_sc[...] = jnp.zeros_like(acc_sc)

    def step(first, width, diagonal=False):
        keys = kv_sc[pl.ds(first, width), :HEAD]
        values = kv_sc[pl.ds(first, width), HEAD:]
        values = jnp.concatenate([values, jnp.ones_like(values)], axis=1)
        scores = []
        for u in range(parts):
            s = lax.dot_general(
                q_ref[u * rows : (u + 1) * rows, :],
                keys,
                (((1,), (1,)), ((), ())),
                preferred_element_type=jnp.float32,
            )
            if diagonal:
                row = lax.broadcasted_iota(jnp.int32, s.shape, 0) + u * rows
                col = lax.broadcasted_iota(jnp.int32, s.shape, 1)
                s = jnp.where(col <= row, s, NEG_FILL)
            scores.append(s)
        for u in range(parts):
            at = slice(u * rows, (u + 1) * rows)
            old = m_sc[at]
            new = jnp.maximum(old, jnp.max(scores[u], axis=1, keepdims=True))
            m_sc[at] = new
            shifted = scores[u] - jnp.tile(new, (1, width // HEAD))
            weights = jnp.exp2(shifted * rate).astype(jnp.bfloat16)
            again = jnp.exp2((old - new) * rate)
            acc_sc[at] = acc_sc[at] * jnp.concatenate([again, again], axis=1) + jnp.dot(
                weights, values, preferred_element_type=jnp.float32
            )

    begin = total - plane - grp * plane

    def earlier(t, _):
        step(pl.multiple_of(begin + t * span, span), span)
        return 0

    lax.fori_loop(0, grp * (plane // span), earlier, 0)
    for i in range(group):
        source = mem ^ i

        @pl.when(source < block)
        def _():
            step(total - plane + i * tok, tok)

        @pl.when(source == block)
        def _():
            step(total - plane + i * tok, tok, True)

    o_ref[...] = (acc_sc[:, :HEAD] / acc_sc[:, HEAD:]).astype(o_ref.dtype)


def attention(place, queries, latents, w, first_head, heads, *, tok, group):
    plane, cols = tok * group, len(latents)
    total, features = latents[0].shape
    n_blocks = plane // tok
    parts = 2 if tok % 32 == 0 else 1
    flops = heads * plane * total * HEAD * 4
    return pl.pallas_call(
        functools.partial(
            attention_kernel,
            cols=cols,
            tok=tok,
            group=group,
            span=plane,
            rate=HEAD**-0.5 * math.log2(math.e),
            parts=parts,
        ),
        out_shape=jax.ShapeDtypeStruct((plane, heads * HEAD), queries.dtype),
        grid_spec=pltpu.PrefetchScalarGridSpec(
            num_scalar_prefetch=1,
            grid=(heads, n_blocks),
            in_specs=[pl.BlockSpec((tok, HEAD), lambda h, j, s: (j, h + first_head))]
            + [
                pl.BlockSpec((total, features), lambda h, j, s: (0, 0), pipeline_mode=pl.Buffered(1))
                for _ in range(cols)
            ]
            + [pl.BlockSpec((cols, features, 2 * HEAD), lambda h, j, s: (0, 0, h + first_head))],
            out_specs=pl.BlockSpec((tok, HEAD), lambda h, j, s: (j, h)),
            scratch_shapes=[
                pltpu.VMEM((total, 2 * HEAD), jnp.bfloat16),
                pltpu.VMEM((tok, HEAD), jnp.float32),
                pltpu.VMEM((tok, 2 * HEAD), jnp.float32),
            ],
        ),
        compiler_params=pltpu.CompilerParams(
            dimension_semantics=("arbitrary", "arbitrary"), vmem_limit_bytes=VMEM_LIMIT
        ),
        cost_estimate=pl.CostEstimate(
            flops=flops, transcendentals=heads * plane * total, bytes_accessed=total * features * cols * 2
        ),
        name="attention",
    )(place, queries, *latents, w)


def project_kernel(order, *refs, pieces, depth):
    a_refs, (b_ref, o_ref) = refs[:pieces], refs[pieces:]
    out = None
    for x in range(pieces):
        at = pl.ds(pl.multiple_of(order[x] * depth, depth), depth)
        term = jnp.dot(a_refs[x][...], b_ref[at, :], preferred_element_type=jnp.float32)
        out = term if out is None else out + term
    o_ref[...] = out.astype(o_ref.dtype)


def project(order, pieces, b, tok):
    rows, depth = pieces[0].shape
    width = b.shape[1]
    return pl.pallas_call(
        functools.partial(project_kernel, pieces=len(pieces), depth=depth),
        out_shape=jax.ShapeDtypeStruct((rows, width), jnp.bfloat16),
        grid_spec=pltpu.PrefetchScalarGridSpec(
            num_scalar_prefetch=1,
            grid=(rows // tok,),
            in_specs=[pl.BlockSpec((tok, depth), lambda j, s: (j, 0)) for _ in pieces]
            + [pl.BlockSpec(b.shape, lambda j, s: (0, 0), pipeline_mode=pl.Buffered(1))],
            out_specs=pl.BlockSpec((tok, width), lambda j, s: (j, 0)),
        ),
        compiler_params=pltpu.CompilerParams(
            dimension_semantics=("arbitrary",), vmem_limit_bytes=VMEM_LIMIT
        ),
        cost_estimate=pl.CostEstimate(
            flops=2 * rows * b.shape[0] * width, transcendentals=0, bytes_accessed=b.size * 2
        ),
        name="project",
    )(order, *pieces, b)


def per_device(latent, w_kv, queries, w_out):
    planes, group, cols = lax.axis_size("grp"), lax.axis_size("mem"), lax.axis_size("col")
    grp, mem, col = lax.axis_index("grp"), lax.axis_index("mem"), lax.axis_index("col")
    tok, features = latent.shape
    plane = tok * group
    per_col = queries.shape[1] // HEAD
    run = w_out.shape[0] // HEAD
    turns = per_col // (group * run)
    place = jnp.stack([grp, mem]).astype(jnp.int32)

    def swap(x, m):
        return lax.ppermute(x, "mem", [(p, p ^ m) for p in range(group)])

    def up(x):
        return lax.ppermute(x, "grp", [(z, z + 1) for z in range(planes - 1)])

    def around(x, k):
        return lax.ppermute(x, "grp", [(z, (z + k) % planes) for z in range(planes)])

    def across(x, s):
        return lax.ppermute(x, "col", [((c + s) % cols, c) for c in range(cols)])

    chain = [latent]
    for _ in range(planes - 1):
        chain.append(up(chain[-1]))
    mine = jnp.stack(chain[::-1])
    whole = jnp.stack([mine] + [swap(mine, m) for m in range(1, group)], axis=1)
    whole = whole.reshape(planes * plane, features)
    latents = [whole] + [across(whole, s) for s in range(1, cols)]

    w_mine = lax.all_to_all(
        w_kv.reshape(w_kv.shape[0], turns, group, run * 2 * HEAD), "mem", 2, 0, tiled=True
    ).reshape(group * w_kv.shape[0], turns * run * 2 * HEAD)
    w_all = jnp.stack([w_mine] + [around(w_mine, k) for k in range(1, planes)])
    w_all = jnp.concatenate(
        [lax.dynamic_index_in_dim(w_all, (grp - z) % planes, 0, False) for z in range(planes)]
    )
    w_rel = jnp.stack(
        [lax.dynamic_slice_in_dim(w_all, ((col + s) % cols) * features, features, 0) for s in range(cols)]
    )

    my_queries = lax.all_to_all(
        queries.reshape(tok, turns, group, run * HEAD), "mem", 2, 0, tiled=True
    ).reshape(plane, turns * run * HEAD)

    w_slice = lax.all_to_all(w_out, "mem", 1, 0, tiled=True)
    w_panel = lax.all_gather(w_slice, "grp", axis=0, tiled=True)

    pieces, order = [], []
    for turn in range(turns):
        own = attention(place, my_queries, latents, w_rel, turn * run, run, tok=tok, group=group)
        for m in range(group):
            part = own if m == 0 else swap(own, m)
            for s in range(cols):
                pieces.append(part if s == 0 else across(part, s))
                order.append((((col + s) % cols) * turns + turn) * group + (mem ^ m))
    mixed = project(jnp.stack(order).astype(jnp.int32), pieces, w_panel, tok)
    return lax.all_to_all(mixed, "mem", 0, 1, tiled=True)


def solution(mesh):
    rows, cols = mesh.devices.shape
    group = 4
    fine = Mesh(mesh.devices.reshape(rows // group, group, cols), ("grp", "mem", "col"))
    spec = P(("grp", "mem"), "col")
    return jax.shard_map(
        per_device, mesh=fine, in_specs=(spec,) * 4, out_specs=spec, check_vma=False
    )
```

```python
import functools
import math

import jax
import jax.numpy as jnp
from jax import lax
from jax.experimental import pallas as pl
from jax.experimental.pallas import tpu as pltpu
from jax.sharding import Mesh, PartitionSpec as P

HEAD = 128
NEG_FILL = -1e30
VMEM_LIMIT = 56 * 1024 * 1024


def attention_kernel(place, q_ref, *refs, cols, rate, parts):
    before, own = refs[:cols], refs[cols : 2 * cols]
    w_ref, o_ref, kv_sc, m_sc, acc_sc = refs[2 * cols :]
    grp = place[0]
    plane = own[0].shape[0]
    earlier = before[0].shape[0]
    block = pl.program_id(1)
    size = q_ref.shape[0]
    rows = size // parts

    def expand(source, at, to):
        out = jnp.dot(source[0][at, :], w_ref[0], preferred_element_type=jnp.float32)
        for s in range(1, cols):
            out += jnp.dot(source[s][at, :], w_ref[s], preferred_element_type=jnp.float32)
        kv_sc[to, :] = out.astype(kv_sc.dtype)

    @pl.when(block == 0)
    def _():
        def plane_before(t, _):
            at = pl.ds(pl.multiple_of(t * plane, plane), plane)
            expand(before, at, at)
            return 0

        lax.fori_loop(earlier // plane - grp, earlier // plane, plane_before, 0)
        expand(own, pl.ds(0, plane), pl.ds(earlier, plane))

    m_sc[...] = jnp.full_like(m_sc, NEG_FILL)
    acc_sc[...] = jnp.zeros_like(acc_sc)

    def step(first, width, query_at=None):
        keys = kv_sc[pl.ds(first, width), :HEAD]
        values = kv_sc[pl.ds(first, width), HEAD:]
        values = jnp.concatenate([values, jnp.ones_like(values)], axis=1)
        scores = []
        for u in range(parts):
            s = lax.dot_general(
                q_ref[u * rows : (u + 1) * rows, :],
                keys,
                (((1,), (1,)), ((), ())),
                preferred_element_type=jnp.float32,
            )
            if query_at is not None:
                row = lax.broadcasted_iota(jnp.int32, s.shape, 0) + (query_at + u * rows)
                col = lax.broadcasted_iota(jnp.int32, s.shape, 1)
                s = jnp.where(col <= row, s, NEG_FILL)
            scores.append(s)
        for u in range(parts):
            at = slice(u * rows, (u + 1) * rows)
            old = m_sc[at]
            new = jnp.maximum(old, jnp.max(scores[u], axis=1, keepdims=True))
            m_sc[at] = new
            shifted = scores[u] - jnp.tile(new, (1, width // HEAD))
            weights = jnp.exp2(shifted * rate).astype(jnp.bfloat16)
            again = jnp.exp2((old - new) * rate)
            acc_sc[at] = acc_sc[at] * jnp.concatenate([again, again], axis=1) + jnp.dot(
                weights, values, preferred_element_type=jnp.float32
            )

    def plane_step(t, _):
        step(pl.multiple_of(t * plane, plane), plane)
        return 0

    for b in range(plane // size):

        @pl.when(block == b)
        def _():
            step(earlier, (b + 1) * size, b * size)

    lax.fori_loop(earlier // plane - grp, earlier // plane, plane_step, 0)
    o_ref[...] = (acc_sc[:, :HEAD] / acc_sc[:, HEAD:]).astype(o_ref.dtype)


def attention(place, queries, before, own, w, first_head, heads):
    cols = len(own)
    plane, features = own[0].shape
    earlier = before[0].shape[0]
    total = earlier + plane
    size = plane // 2
    fixed = lambda h, j, s: (0, 0)
    return pl.pallas_call(
        functools.partial(
            attention_kernel, cols=cols, rate=HEAD**-0.5 * math.log2(math.e), parts=2
        ),
        out_shape=jax.ShapeDtypeStruct((plane, heads * HEAD), queries.dtype),
        grid_spec=pltpu.PrefetchScalarGridSpec(
            num_scalar_prefetch=1,
            grid=(heads, plane // size),
            in_specs=[pl.BlockSpec((size, HEAD), lambda h, j, s: (j, h + first_head))]
            + [pl.BlockSpec((earlier, features), fixed, pipeline_mode=pl.Buffered(1)) for _ in before]
            + [pl.BlockSpec((plane, features), fixed, pipeline_mode=pl.Buffered(1)) for _ in own]
            + [pl.BlockSpec((cols, features, 2 * HEAD), lambda h, j, s: (0, 0, h + first_head))],
            out_specs=pl.BlockSpec((size, HEAD), lambda h, j, s: (j, h)),
            scratch_shapes=[
                pltpu.VMEM((total, 2 * HEAD), jnp.bfloat16),
                pltpu.VMEM((size, HEAD), jnp.float32),
                pltpu.VMEM((size, 2 * HEAD), jnp.float32),
            ],
        ),
        compiler_params=pltpu.CompilerParams(
            dimension_semantics=("arbitrary", "arbitrary"), vmem_limit_bytes=VMEM_LIMIT
        ),
        cost_estimate=pl.CostEstimate(
            flops=heads * plane * total * HEAD * 6,
            transcendentals=heads * plane * total,
            bytes_accessed=total * features * cols * 2,
        ),
        name="attention",
    )(place, queries, *before, *own, w)


def project_kernel(scalars, *refs, pieces, shifts, group, carried, last):
    a_refs, refs = refs[:pieces], refs[pieces:]
    b_refs, refs = refs[: len(shifts)], refs[len(shifts) :]
    if carried:
        part_ref, refs = refs[0], refs[1:]
    outs, (b_sc, acc_sc, sems) = refs[:-3], refs[-3:]
    step = pl.program_id(0)
    depth = a_refs[0].shape[1]
    copies = [pltpu.make_async_copy(b_refs[i], b_sc.at[i], sems.at[i]) for i in range(len(shifts))]

    @pl.when(step == 0)
    def _():
        for copy in copies:
            copy.start()
        for copy in copies:
            copy.wait()

    if carried:
        acc_sc[...] = part_ref[...]
    else:
        acc_sc[...] = jnp.zeros_like(acc_sc)
    for x in range(0, pieces, group):
        for i, shift in enumerate(shifts):

            @pl.when(scalars[x // group] == shift)
            def _():
                out = acc_sc[...]
                for m in range(group):
                    rows = b_sc[i, m * depth : (m + 1) * depth, :]
                    out = out + jnp.dot(a_refs[x + m][...], rows, preferred_element_type=jnp.float32)
                acc_sc[...] = out

    if last:
        for m in range(group):

            @pl.when(step == m)
            def _():
                outs[m][...] = acc_sc[...].astype(outs[m].dtype)
    else:
        outs[0][...] = acc_sc[...]


def project(scalars, pieces, blocks, shifts, carried, first, group, last):
    rows, depth = pieces[0].shape
    tok = rows // group
    count = len(scalars_of(pieces, group))
    width = blocks[0].shape[1]
    outs = (
        [jax.ShapeDtypeStruct((tok, width), jnp.bfloat16)] * group
        if last
        else [jax.ShapeDtypeStruct((rows, width), jnp.float32)]
    )
    in_specs = [pl.BlockSpec((tok, depth), lambda j, s: (s[count] ^ j, 0)) for _ in pieces]
    in_specs += [pl.BlockSpec(memory_space=pl.ANY) for _ in blocks]
    operands = [*pieces, *blocks]
    if carried is not None:
        in_specs.append(pl.BlockSpec((tok, width), lambda j, s: (j, first // width)))
        operands.append(carried)
    return pl.pallas_call(
        functools.partial(
            project_kernel,
            pieces=len(pieces),
            shifts=shifts,
            group=group,
            carried=carried is not None,
            last=last,
        ),
        out_shape=outs,
        grid_spec=pltpu.PrefetchScalarGridSpec(
            num_scalar_prefetch=1,
            grid=(group,),
            in_specs=in_specs,
            out_specs=[pl.BlockSpec((tok, width), lambda j, s: (0, 0))] * group
            if last
            else [pl.BlockSpec((tok, width), lambda j, s: (j, 0))],
            scratch_shapes=[
                pltpu.VMEM((len(blocks), *blocks[0].shape), jnp.bfloat16),
                pltpu.VMEM((tok, width), jnp.float32),
                pltpu.SemaphoreType.DMA((len(blocks),)),
            ],
        ),
        compiler_params=pltpu.CompilerParams(
            dimension_semantics=("arbitrary",), vmem_limit_bytes=VMEM_LIMIT
        ),
        cost_estimate=pl.CostEstimate(
            flops=2 * rows * len(blocks) * blocks[0].shape[0] * width,
            transcendentals=0,
            bytes_accessed=len(blocks) * blocks[0].size * 2 + rows * depth * len(pieces) * 2,
        ),
        name="project",
    )(scalars, *operands)


def scalars_of(pieces, group):
    return range(len(pieces) // group)


def per_device(latent, w_kv, queries, w_out):
    planes, group, cols = lax.axis_size("grp"), lax.axis_size("mem"), lax.axis_size("col")
    grp, mem, col = lax.axis_index("grp"), lax.axis_index("mem"), lax.axis_index("col")
    tok, features = latent.shape
    plane = tok * group
    per_col = queries.shape[1] // HEAD
    run = w_out.shape[0] // HEAD
    turns = per_col // (group * run)
    place = jnp.stack([grp, mem]).astype(jnp.int32)

    def swap(x, m):
        return lax.ppermute(x, "mem", [(p, p ^ m) for p in range(group)])

    def up(x, k):
        return lax.ppermute(x, "grp", [(z, z + k) for z in range(planes - k)])

    def across(x, s):
        return lax.ppermute(x, "col", [((c + s) % cols, c) for c in range(cols)])

    def plane_swap(x, k, pairs=None):
        pairs = range(planes) if pairs is None else pairs
        return lax.ppermute(x, "grp", [(z, z ^ k) for z in pairs])

    near = [z for z in range(planes) if abs(z - (z ^ (planes - 1))) == 1]
    far = [z for z in range(planes) if z not in near]
    half = planes // 2

    def pick(stack, index):
        return lax.dynamic_index_in_dim(stack, index, 0, False)

    def other_planes(x):
        got = {k: plane_swap(x, k) for k in range(1, planes - 1)}
        direct = plane_swap(x, planes - 1, near)
        last = (planes - 1) ^ half
        relayed = plane_swap(got[half], last, [z ^ last for z in far])
        is_near = functools.reduce(jnp.logical_or, [grp == z for z in near])
        return got, direct, relayed, is_near

    width = w_out.shape[1] // group
    cut = w_out.reshape(w_out.shape[0], group, width)
    w_slice = jnp.concatenate(
        [lax.dynamic_index_in_dim(cut, mem, 1, False)]
        + [swap(lax.dynamic_index_in_dim(cut, mem ^ m, 1, False), m) for m in range(1, group)]
    )

    chips = jnp.stack([latent] + [swap(latent, m) for m in range(1, group)])
    own = jnp.concatenate([pick(chips, mem ^ p) for p in range(group)])
    lower = [up(latent, k) for k in range(planes - 1, 0, -1)]

    w_cut = w_kv.reshape(w_kv.shape[0], turns, group, run * 2 * HEAD)
    w_mine = jnp.stack(
        [lax.dynamic_index_in_dim(w_cut, mem, 2, False)]
        + [swap(lax.dynamic_index_in_dim(w_cut, mem ^ m, 2, False), m) for m in range(1, group)]
    )

    w_slice, lower, queries, w_mine = lax.optimization_barrier((w_slice, lower, queries, w_mine))
    got, direct, relayed, is_near = other_planes(w_slice)

    below = jnp.stack(lower)
    below = jnp.stack([below] + [swap(below, m) for m in range(1, group)], axis=1)
    below = below.reshape((planes - 1) * plane, features)
    w_got, w_direct, w_relayed, _ = other_planes(w_mine)
    w_got[planes - 1] = jnp.where(is_near, w_direct, w_relayed)
    w_all = jnp.stack([w_mine] + [w_got[k] for k in range(1, planes)]).reshape(
        planes * group, w_kv.shape[0], turns * run * 2 * HEAD
    )
    w_all = jnp.concatenate(
        [pick(w_all, (grp ^ z) * group + (mem ^ p)) for z in range(planes) for p in range(group)]
    )
    w_rel = jnp.stack(
        [lax.dynamic_slice_in_dim(w_all, ((col + s) % cols) * features, features, 0) for s in range(cols)]
    )
    q_cut = queries.reshape(tok, turns, group, run * HEAD)
    q_got = jnp.stack(
        [lax.dynamic_index_in_dim(q_cut, mem, 2, False)]
        + [swap(lax.dynamic_index_in_dim(q_cut, mem ^ m, 2, False), m) for m in range(1, group)]
    ).reshape(group, tok, turns * run * HEAD)
    my_queries = jnp.concatenate([pick(q_got, mem ^ p) for p in range(group)])

    befores = [below] + [across(below, s) for s in range(1, cols)]
    owns = [own] + [across(own, s) for s in range(1, cols)]

    pieces, shifts = [], []
    for turn in range(turns):
        done = attention(place, my_queries, befores, owns, w_rel, turn * run, run)
        parts = [done] + [swap(done, m) for m in range(1, group)]
        for s in range(cols):
            pieces += [part if s == 0 else across(part, s) for part in parts]
            shifts.append((((col + s) % cols) * turns + turn) ^ grp)
    scalars = jnp.stack(shifts + [mem]).astype(jnp.int32)
    near_shifts = list(range(planes - 1))
    partial = project(
        scalars, pieces, [w_slice] + [got[k] for k in near_shifts[1:]], near_shifts, None, 0, group, False
    )[0]
    farthest = jnp.where(is_near, direct, relayed)
    mixed = project(scalars, pieces, [farthest], [planes - 1], partial, 0, group, True)
    mixed = jnp.stack([mixed[0]] + [swap(mixed[m], m) for m in range(1, group)])
    return jnp.concatenate([pick(mixed, mem ^ p) for p in range(group)], axis=1)


def solution(mesh):
    rows, cols = mesh.devices.shape
    group = 4
    fine = Mesh(mesh.devices.reshape(rows // group, group, cols), ("grp", "mem", "col"))
    spec = P(("grp", "mem"), "col")
    return jax.shard_map(
        per_device, mesh=fine, in_specs=(spec,) * 4, out_specs=spec, check_vma=False
    )
```

```python
import functools
import math

import jax
import jax.numpy as jnp
from jax import lax
from jax.experimental import pallas as pl
from jax.experimental.pallas import tpu as pltpu
from jax.sharding import Mesh, PartitionSpec as P

HEAD = 128
NEG_FILL = -1e30
VMEM_LIMIT = 56 * 1024 * 1024


def cut_kernel(place, *refs, takes):
    ins, outs = refs[: len(takes)], refs[len(takes) :]
    mem = place[1]
    at = 0
    for ref, take in zip(ins, takes):
        for m, stride, parts in take:
            done = 0
            for offset, width in parts:
                first = pl.multiple_of((mem ^ m) * stride + offset, HEAD)
                outs[at][:, done : done + width] = ref[:, pl.ds(first, width)]
                done += width
            at += 1


def cut(place, arrays, takes):
    flat = [(x, take) for x, some in zip(arrays, takes) for take in some]
    widths = [n for _, (_, stride, parts) in flat for n in (stride, *(v for p in parts for v in p))]
    if any(n % HEAD for n in widths):
        mem = place[1]
        return [
            jnp.concatenate(
                [lax.dynamic_slice_in_dim(x, (mem ^ m) * stride + o, n, 1) for o, n in parts], axis=1
            )
            for x, (m, stride, parts) in flat
        ]
    return pl.pallas_call(
        functools.partial(cut_kernel, takes=takes),
        out_shape=[
            jax.ShapeDtypeStruct((x.shape[0], sum(n for _, n in parts)), x.dtype)
            for x, (_, _, parts) in flat
        ],
        grid_spec=pltpu.PrefetchScalarGridSpec(
            num_scalar_prefetch=1,
            grid=(1,),
            in_specs=[pl.BlockSpec(x.shape, lambda i, s: (0, 0)) for x in arrays],
            out_specs=[
                pl.BlockSpec((x.shape[0], sum(n for _, n in parts)), lambda i, s: (0, 0))
                for x, (_, _, parts) in flat
            ],
        ),
        compiler_params=pltpu.CompilerParams(vmem_limit_bytes=VMEM_LIMIT),
        cost_estimate=pl.CostEstimate(
            flops=0, transcendentals=0, bytes_accessed=2 * sum(2 * x.size for x in arrays)
        ),
        name="cut",
    )(place, *arrays)


def attention_kernel(place, *refs, planes, group, cols, rate, parts):
    q_refs, refs = refs[:group], refs[group:]
    own, refs = refs[: cols * group], refs[cols * group :]
    before, refs = refs[: cols * group], refs[cols * group :]
    w_refs, refs = refs[:planes], refs[planes:]
    o_ref, q_sc, w_sc, kv_sc, m_sc, acc_sc = refs
    grp, mem, col = place[0], place[1], place[2]
    tok, features = own[0].shape
    plane = tok * group
    earlier = (planes - 1) * plane
    block = pl.program_id(1)
    size = o_ref.shape[0]
    rows = size // parts
    depth = w_refs[0].shape[1]

    def expand(sources, at, to):
        out = None
        for s in range(cols):
            w = w_sc[pl.ds(pl.multiple_of(((col + s) % cols) * features, features), features), :]
            term = jnp.dot(sources[s * group][at, :], w, preferred_element_type=jnp.float32)
            out = term if out is None else out + term
        kv_sc[to, :] = out.astype(kv_sc.dtype)

    @pl.when(block == 0)
    def _():
        for m in range(group):
            q_sc[pl.ds(pl.multiple_of((mem ^ m) * tok, tok), tok), :] = q_refs[m][...]
            for k in range(planes):
                first = ((grp ^ k) * group + (mem ^ m)) * depth
                w_sc[pl.ds(pl.multiple_of(first, depth), depth), :] = w_refs[k][m]
        for m in range(group):
            first = earlier + (mem ^ m) * tok
            expand(own[m:], pl.ds(0, tok), pl.ds(pl.multiple_of(first, tok), tok))

        def plane_before(t, _):
            for m in range(group):
                at = pl.ds(pl.multiple_of(t * tok, tok), tok)
                expand(before[m:], at, pl.ds(pl.multiple_of(t * plane + m * tok, tok), tok))
            return 0

        lax.fori_loop(planes - 1 - grp, planes - 1, plane_before, 0)

    m_sc[...] = jnp.full_like(m_sc, NEG_FILL)
    acc_sc[...] = jnp.zeros_like(acc_sc)
    base = pl.multiple_of(block * size, size)

    def step(first, width, query_at=None):
        keys = kv_sc[pl.ds(first, width), :HEAD]
        values = kv_sc[pl.ds(first, width), HEAD:]
        values = jnp.concatenate([values, jnp.ones_like(values)], axis=1)
        scores = []
        for u in range(parts):
            s = lax.dot_general(
                q_sc[pl.ds(base + u * rows, rows), :],
                keys,
                (((1,), (1,)), ((), ())),
                preferred_element_type=jnp.float32,
            )
            if query_at is not None:
                row = lax.broadcasted_iota(jnp.int32, s.shape, 0) + (query_at + u * rows)
                column = lax.broadcasted_iota(jnp.int32, s.shape, 1)
                s = jnp.where(column <= row, s, NEG_FILL)
            scores.append(s)
        for u in range(parts):
            at = slice(u * rows, (u + 1) * rows)
            old = m_sc[at]
            new = jnp.maximum(old, jnp.max(scores[u], axis=1, keepdims=True))
            m_sc[at] = new
            shifted = scores[u] - jnp.tile(new, (1, width // HEAD))
            weights = jnp.exp2(shifted * rate).astype(jnp.bfloat16)
            again = jnp.exp2((old - new) * rate)
            acc_sc[at] = acc_sc[at] * jnp.concatenate([again, again], axis=1) + jnp.dot(
                weights, values, preferred_element_type=jnp.float32
            )

    def plane_step(t, _):
        step(pl.multiple_of(t * plane, plane), plane)
        return 0

    for b in range(plane // size):

        @pl.when(block == b)
        def _():
            step(earlier, (b + 1) * size, b * size)

    lax.fori_loop(planes - 1 - grp, planes - 1, plane_step, 0)
    o_ref[...] = (acc_sc[:, :HEAD] / acc_sc[:, HEAD:]).astype(o_ref.dtype)


def attention(place, queries, own, before, w, first_head, heads):
    planes, group, cols = len(w), len(queries), len(own)
    tok, features = own[0][0].shape
    plane = tok * group
    total = planes * plane
    size = plane // 2
    fixed = lambda h, j, s: (0, 0)
    whole = [pl.BlockSpec(x.shape, fixed, pipeline_mode=pl.Buffered(1)) for x in own[0] * cols]
    whole += [pl.BlockSpec(x.shape, fixed, pipeline_mode=pl.Buffered(1)) for x in before[0] * cols]
    return pl.pallas_call(
        functools.partial(
            attention_kernel,
            planes=planes,
            group=group,
            cols=cols,
            rate=HEAD**-0.5 * math.log2(math.e),
            parts=2,
        ),
        out_shape=jax.ShapeDtypeStruct((plane, heads * HEAD), jnp.bfloat16),
        grid_spec=pltpu.PrefetchScalarGridSpec(
            num_scalar_prefetch=1,
            grid=(heads, plane // size),
            in_specs=[pl.BlockSpec((tok, HEAD), lambda h, j, s: (0, h + first_head)) for _ in queries]
            + whole
            + [
                pl.BlockSpec((*x.shape[:2], 2 * HEAD), lambda h, j, s: (0, 0, h + first_head)) for x in w
            ],
            out_specs=pl.BlockSpec((size, HEAD), lambda h, j, s: (j, h)),
            scratch_shapes=[
                pltpu.VMEM((plane, HEAD), jnp.bfloat16),
                pltpu.VMEM((features * cols, 2 * HEAD), jnp.bfloat16),
                pltpu.VMEM((total, 2 * HEAD), jnp.bfloat16),
                pltpu.VMEM((size, HEAD), jnp.float32),
                pltpu.VMEM((size, 2 * HEAD), jnp.float32),
            ],
        ),
        compiler_params=pltpu.CompilerParams(
            dimension_semantics=("arbitrary", "arbitrary"), vmem_limit_bytes=VMEM_LIMIT
        ),
        cost_estimate=pl.CostEstimate(
            flops=heads * plane * total * HEAD * 6,
            transcendentals=heads * plane * total,
            bytes_accessed=total * features * cols * 2,
        ),
        name="attention",
    )(place, *queries, *(x for some in own for x in some), *(x for some in before for x in some), *w)


def project_kernel(scalars, *refs, counts, group, planes):
    a_refs, refs = refs[: sum(counts)], refs[sum(counts) :]
    b_refs, refs = refs[: planes + 1], refs[planes + 1 :]
    outs, (b_sc, sems) = refs[:group], refs[group:]
    step = pl.program_id(0)
    near = scalars[len(counts) + 1] == 1

    @pl.when(step == 0)
    def _():
        copies = [pltpu.make_async_copy(b_refs[k], b_sc.at[k], sems.at[k]) for k in range(planes - 1)]
        for copy in copies:
            copy.start()
        for which, source in ((near, b_refs[planes - 1]), (jnp.logical_not(near), b_refs[planes])):

            @pl.when(which)
            def _():
                copy = pltpu.make_async_copy(source, b_sc.at[planes - 1], sems.at[planes - 1])
                copy.start()
                copy.wait()

        for copy in copies:
            copy.wait()

    out, at = None, 0
    for x, count in enumerate(counts):
        heads = [a_refs[at + i][...] for i in range(count)]
        a = heads[0] if count == 1 else jnp.concatenate(heads, axis=1)
        term = jnp.dot(a, b_sc[scalars[x]], preferred_element_type=jnp.float32)
        out = term if out is None else out + term
        at += count
    for m in range(group):

        @pl.when(step == m)
        def _():
            outs[m][...] = out.astype(outs[m].dtype)


def project(scalars, sets, blocks, group):
    pieces = [x for some in sets for x in some]
    planes = len(blocks) - 1
    tok = pieces[0].shape[0] // group
    depth, width = blocks[0].shape
    count = len(sets)
    return pl.pallas_call(
        functools.partial(
            project_kernel, counts=[len(some) for some in sets], group=group, planes=planes
        ),
        out_shape=[jax.ShapeDtypeStruct((tok, width), jnp.bfloat16)] * group,
        grid_spec=pltpu.PrefetchScalarGridSpec(
            num_scalar_prefetch=1,
            grid=(group,),
            in_specs=[
                pl.BlockSpec((tok, x.shape[1]), lambda j, s: (s[count] ^ j, 0)) for x in pieces
            ]
            + [pl.BlockSpec(memory_space=pl.ANY) for _ in blocks],
            out_specs=[pl.BlockSpec((tok, width), lambda j, s: (0, 0))] * group,
            scratch_shapes=[
                pltpu.VMEM((planes, depth, width), jnp.bfloat16),
                pltpu.SemaphoreType.DMA((planes,)),
            ],
        ),
        compiler_params=pltpu.CompilerParams(
            dimension_semantics=("arbitrary",), vmem_limit_bytes=VMEM_LIMIT
        ),
        cost_estimate=pl.CostEstimate(
            flops=2 * tok * group * planes * depth * width,
            transcendentals=0,
            bytes_accessed=planes * depth * width * 2 + tok * group * planes * depth * 2,
        ),
        name="project",
    )(scalars, *pieces, *blocks)


def per_device(latent, w_kv, queries, w_out):
    planes, group, cols = lax.axis_size("grp"), lax.axis_size("mem"), lax.axis_size("col")
    grp, mem, col = lax.axis_index("grp"), lax.axis_index("mem"), lax.axis_index("col")
    tok, features = latent.shape
    per_col = queries.shape[1] // HEAD
    run = w_out.shape[0] // HEAD
    turns = per_col // (group * run)
    place = jnp.stack([grp, mem, col]).astype(jnp.int32)
    shifts = range(group)

    def swap(x, m):
        return lax.ppermute(x, "mem", [(p, p ^ m) for p in range(group)])

    def gather(x):
        return [x] + [swap(x, m) for m in range(1, group)]

    def exchange(xs):
        return [xs[0]] + [swap(xs[m], m) for m in range(1, group)]

    def up(x, k):
        return lax.ppermute(x, "grp", [(z, z + k) for z in range(planes - k)])

    def across(x, s):
        return lax.ppermute(x, "col", [((c + s) % cols, c) for c in range(cols)])

    def plane_swap(x, k, senders=None):
        senders = range(planes) if senders is None else senders
        return lax.ppermute(x, "grp", [(z, z ^ k) for z in senders])

    far_shift, half = planes - 1, planes // 2
    near = [z for z in range(planes) if abs(z - (z ^ far_shift)) == 1]
    far = [z for z in range(planes) if z not in near]
    is_near = functools.reduce(jnp.logical_or, [grp == z for z in near]).astype(jnp.int32)

    def relay(x):
        last = far_shift ^ half
        return plane_swap(x, last, [z ^ last for z in far])

    width = w_out.shape[1] // group
    first_width = -(-width // (2 * HEAD)) * HEAD
    spans = [(0, first_width), (first_width, width - first_width)]

    def by_turn(n):
        return [(m, n, [(t * group * n, n) for t in range(turns)]) for m in shifts]

    takes = [
        by_turn(run * 2 * HEAD),
        [(m, width, [span]) for span in spans for m in shifts],
        by_turn(run * HEAD),
    ]
    blocks = cut(place, [w_kv, w_out, queries], takes)
    w_mine = exchange(blocks[:group])
    lower = [up(latent, k) for k in range(planes - 1, 0, -1)]
    own = gather(latent)
    w_first = exchange(blocks[group : 2 * group])

    w_mine = jnp.stack(w_mine)
    w_all = [w_mine] + [plane_swap(w_mine, k) for k in range(1, planes)]

    def spread(x):
        x = jnp.concatenate(x)
        return [x] + [plane_swap(x, k) for k in (half, *(k for k in range(1, far_shift) if k != half))] + [
            plane_swap(x, far_shift, near)
        ]

    out_first = spread(w_first)
    q_send, lower, _ = lax.optimization_barrier((blocks[3 * group :], lower, w_first[1:]))
    below = gather(jnp.concatenate(lower))
    my_queries = exchange(q_send)
    w_send, _ = lax.optimization_barrier((blocks[2 * group : 3 * group], my_queries))
    w_second = exchange(w_send)

    owns = [own] + [[across(x, s) for x in own] for s in range(1, cols)]
    belows = [below] + [[across(x, s) for x in below] for s in range(1, cols)]

    calls = [(t, t * run, run) for t in range(turns - 1)]
    calls += [((turns - 1), (turns - 1) * run + i, 1) for i in range(run)]
    results = [[] for _ in range(turns)]
    done = []
    for turn, first_head, heads in calls:
        out = attention(place, my_queries, owns, belows, w_all, first_head, heads)
        done.append(out)
        results[turn].append(gather(out))
        if len(done) == 1:
            middle, _ = lax.optimization_barrier((out_first[1], out))
            first_far = relay(middle)
            w_second, _ = lax.optimization_barrier((w_second, out))
            out_second = spread(w_second)
    middle, _ = lax.optimization_barrier((out_second[1], done[-1]))
    second_far = relay(middle)

    sets, meets = [], []
    for turn in range(turns):
        for s in range(cols):
            some = [[x if s == 0 else across(x, s) for x in part] for part in results[turn]]
            sets.append([part[m] for m in shifts for part in some])
            meets.append((((col + s) % cols) * turns + turn) ^ grp)
    scalars = jnp.stack([*meets, mem, is_near]).astype(jnp.int32)

    def in_order(out, last):
        by_shift = {0: out[0], half: out[1], far_shift: out[-1]}
        by_shift.update(zip((k for k in range(1, far_shift) if k != half), out[2:-1]))
        return [by_shift[k] for k in range(planes)] + [last]

    mixed = []
    for out, last in ((out_first, first_far), (out_second, second_far)):
        got = exchange(project(scalars, sets, in_order(out, last), group))
        stack = jnp.stack(got)
        mixed.append([lax.dynamic_index_in_dim(stack, mem ^ p, 0, False) for p in shifts])
    return jnp.concatenate([part[p] for p in shifts for part in mixed], axis=1)


def solution(mesh):
    rows, cols = mesh.devices.shape
    group = 4
    fine = Mesh(mesh.devices.reshape(rows // group, group, cols), ("grp", "mem", "col"))
    spec = P(("grp", "mem"), "col")
    return jax.shard_map(
        per_device, mesh=fine, in_specs=(spec,) * 4, out_specs=spec, check_vma=False
    )
```

```python
import functools
import math

import jax
import jax.numpy as jnp
from jax import lax
from jax.experimental import pallas as pl
from jax.experimental.pallas import tpu as pltpu
from jax.sharding import Mesh, PartitionSpec as P


HEAD = 128
NEG_FILL = -1e30
VMEM_LIMIT = 56 * 1024 * 1024


def cut_kernel(place, *refs, takes):
    ins, outs = refs[: len(takes)], refs[len(takes) :]
    mem = place[1]
    at = 0
    for ref, take in zip(ins, takes):
        for m, stride, parts in take:
            done = 0
            for offset, width in parts:
                first = pl.multiple_of((mem ^ m) * stride + offset, HEAD)
                outs[at][:, done : done + width] = ref[:, pl.ds(first, width)]
                done += width
            at += 1


def cut(place, arrays, takes):
    flat = [(x, take) for x, some in zip(arrays, takes) for take in some]
    widths = [n for _, (_, stride, parts) in flat for n in (stride, *(v for p in parts for v in p))]
    if any(n % HEAD for n in widths):
        mem = place[1]
        return [
            jnp.concatenate(
                [lax.dynamic_slice_in_dim(x, (mem ^ m) * stride + o, n, 1) for o, n in parts], axis=1
            )
            for x, (m, stride, parts) in flat
        ]
    return pl.pallas_call(
        functools.partial(cut_kernel, takes=takes),
        out_shape=[
            jax.ShapeDtypeStruct((x.shape[0], sum(n for _, n in parts)), x.dtype)
            for x, (_, _, parts) in flat
        ],
        grid_spec=pltpu.PrefetchScalarGridSpec(
            num_scalar_prefetch=1,
            grid=(1,),
            in_specs=[pl.BlockSpec(x.shape, lambda i, s: (0, 0)) for x in arrays],
            out_specs=[
                pl.BlockSpec((x.shape[0], sum(n for _, n in parts)), lambda i, s: (0, 0))
                for x, (_, _, parts) in flat
            ],
        ),
        compiler_params=pltpu.CompilerParams(vmem_limit_bytes=VMEM_LIMIT),
        cost_estimate=pl.CostEstimate(
            flops=0, transcendentals=0, bytes_accessed=2 * sum(2 * x.size for x in arrays)
        ),
        name="cut",
    )(place, *arrays)


def attention_kernel(place, *refs, planes, group, cols, rate, parts):
    q_refs, refs = refs[:group], refs[group:]
    own, refs = refs[: cols * group], refs[cols * group :]
    before, refs = refs[: cols * group], refs[cols * group :]
    w_refs, refs = refs[:planes], refs[planes:]
    o_ref, q_sc, w_sc, kv_sc, m_sc, acc_sc = refs
    grp, mem, col = place[0], place[1], place[2]
    tok, features = own[0].shape
    plane = tok * group
    earlier = (planes - 1) * plane
    block = pl.program_id(1)
    size = o_ref.shape[0]
    rows = size // parts
    depth = w_refs[0].shape[1]

    def expand(sources, at, to):
        out = None
        for s in range(cols):
            w = w_sc[pl.ds(pl.multiple_of(((col + s) % cols) * features, features), features), :]
            term = jnp.dot(sources[s * group][at, :], w, preferred_element_type=jnp.float32)
            out = term if out is None else out + term
        kv_sc[to, :] = out.astype(kv_sc.dtype)

    @pl.when(block == 0)
    def _():
        for m in range(group):
            q_sc[pl.ds(pl.multiple_of((mem ^ m) * tok, tok), tok), :] = q_refs[m][...]
            for k in range(planes):
                first = ((grp ^ k) * group + (mem ^ m)) * depth
                w_sc[pl.ds(pl.multiple_of(first, depth), depth), :] = w_refs[k][m]
        for m in range(group):
            first = earlier + (mem ^ m) * tok
            expand(own[m:], pl.ds(0, tok), pl.ds(pl.multiple_of(first, tok), tok))

        def plane_before(t, _):
            for m in range(group):
                at = pl.ds(pl.multiple_of(t * tok, tok), tok)
                expand(before[m:], at, pl.ds(pl.multiple_of(t * plane + m * tok, tok), tok))
            return 0

        lax.fori_loop(planes - 1 - grp, planes - 1, plane_before, 0)

    m_sc[...] = jnp.full_like(m_sc, NEG_FILL)
    acc_sc[...] = jnp.zeros_like(acc_sc)
    base = pl.multiple_of(block * size, size)

    def step(first, width, query_at=None):
        keys = kv_sc[pl.ds(first, width), :HEAD]
        values = kv_sc[pl.ds(first, width), HEAD:]
        values = jnp.concatenate([values, jnp.ones_like(values)], axis=1)
        scores = []
        for u in range(parts):
            s = lax.dot_general(
                q_sc[pl.ds(base + u * rows, rows), :],
                keys,
                (((1,), (1,)), ((), ())),
                preferred_element_type=jnp.float32,
            )
            if query_at is not None:
                row = lax.broadcasted_iota(jnp.int32, s.shape, 0) + (query_at + u * rows)
                column = lax.broadcasted_iota(jnp.int32, s.shape, 1)
                s = jnp.where(column <= row, s, NEG_FILL)
            scores.append(s)
        for u in range(parts):
            at = slice(u * rows, (u + 1) * rows)
            old = m_sc[at]
            new = jnp.maximum(old, jnp.max(scores[u], axis=1, keepdims=True))
            m_sc[at] = new
            shifted = scores[u] - jnp.tile(new, (1, width // HEAD))
            weights = jnp.exp2(shifted * rate).astype(jnp.bfloat16)
            again = jnp.exp2((old - new) * rate)
            acc_sc[at] = acc_sc[at] * jnp.concatenate([again, again], axis=1) + jnp.dot(
                weights, values, preferred_element_type=jnp.float32
            )

    def plane_step(t, _):
        step(pl.multiple_of(t * plane, plane), plane)
        return 0

    for b in range(plane // size):

        @pl.when(block == b)
        def _():
            step(earlier, (b + 1) * size, b * size)

    lax.fori_loop(planes - 1 - grp, planes - 1, plane_step, 0)
    o_ref[...] = (acc_sc[:, :HEAD] / acc_sc[:, HEAD:]).astype(o_ref.dtype)


def attention(place, queries, own, before, w, first_head, heads):
    planes, group, cols = len(w), len(queries), len(own)
    tok, features = own[0][0].shape
    plane = tok * group
    total = planes * plane
    size = plane // 2
    fixed = lambda h, j, s: (0, 0)
    whole = [pl.BlockSpec(x.shape, fixed, pipeline_mode=pl.Buffered(1)) for x in own[0] * cols]
    whole += [pl.BlockSpec(x.shape, fixed, pipeline_mode=pl.Buffered(1)) for x in before[0] * cols]
    return pl.pallas_call(
        functools.partial(
            attention_kernel,
            planes=planes,
            group=group,
            cols=cols,
            rate=HEAD**-0.5 * math.log2(math.e),
            parts=2,
        ),
        out_shape=jax.ShapeDtypeStruct((plane, heads * HEAD), jnp.bfloat16),
        grid_spec=pltpu.PrefetchScalarGridSpec(
            num_scalar_prefetch=1,
            grid=(heads, plane // size),
            in_specs=[pl.BlockSpec((tok, HEAD), lambda h, j, s: (0, h + first_head)) for _ in queries]
            + whole
            + [
                pl.BlockSpec((*x.shape[:2], 2 * HEAD), lambda h, j, s: (0, 0, h + first_head)) for x in w
            ],
            out_specs=pl.BlockSpec((size, HEAD), lambda h, j, s: (j, h)),
            scratch_shapes=[
                pltpu.VMEM((plane, HEAD), jnp.bfloat16),
                pltpu.VMEM((features * cols, 2 * HEAD), jnp.bfloat16),
                pltpu.VMEM((total, 2 * HEAD), jnp.bfloat16),
                pltpu.VMEM((size, HEAD), jnp.float32),
                pltpu.VMEM((size, 2 * HEAD), jnp.float32),
            ],
        ),
        compiler_params=pltpu.CompilerParams(
            dimension_semantics=("arbitrary", "arbitrary"), vmem_limit_bytes=VMEM_LIMIT
        ),
        cost_estimate=pl.CostEstimate(
            flops=heads * plane * total * HEAD * 6,
            transcendentals=heads * plane * total,
            bytes_accessed=total * features * cols * 2,
        ),
        name="attention",
    )(place, *queries, *(x for some in own for x in some), *(x for some in before for x in some), *w)


def project_kernel(scalars, *refs, counts, group, planes):
    a_refs, refs = refs[: sum(counts)], refs[sum(counts) :]
    b_refs, refs = refs[: planes + 1], refs[planes + 1 :]
    outs, (b_sc, sems) = refs[:group], refs[group:]
    step = pl.program_id(0)
    near = scalars[len(counts) + 1] == 1

    @pl.when(step == 0)
    def _():
        copies = [pltpu.make_async_copy(b_refs[k], b_sc.at[k], sems.at[k]) for k in range(planes - 1)]
        for copy in copies:
            copy.start()
        for which, source in ((near, b_refs[planes - 1]), (jnp.logical_not(near), b_refs[planes])):

            @pl.when(which)
            def _():
                copy = pltpu.make_async_copy(source, b_sc.at[planes - 1], sems.at[planes - 1])
                copy.start()
                copy.wait()

        for copy in copies:
            copy.wait()

    out, at = None, 0
    for x, count in enumerate(counts):
        heads = [a_refs[at + i][...] for i in range(count)]
        a = heads[0] if count == 1 else jnp.concatenate(heads, axis=1)
        term = jnp.dot(a, b_sc[scalars[x]], preferred_element_type=jnp.float32)
        out = term if out is None else out + term
        at += count
    for m in range(group):

        @pl.when(step == m)
        def _():
            outs[m][...] = out.astype(outs[m].dtype)


def project(scalars, sets, blocks, group):
    pieces = [x for some in sets for x in some]
    planes = len(blocks) - 1
    tok = pieces[0].shape[0] // group
    depth, width = blocks[0].shape
    count = len(sets)
    return pl.pallas_call(
        functools.partial(
            project_kernel, counts=[len(some) for some in sets], group=group, planes=planes
        ),
        out_shape=[jax.ShapeDtypeStruct((tok, width), jnp.bfloat16)] * group,
        grid_spec=pltpu.PrefetchScalarGridSpec(
            num_scalar_prefetch=1,
            grid=(group,),
            in_specs=[
                pl.BlockSpec((tok, x.shape[1]), lambda j, s: (s[count] ^ j, 0)) for x in pieces
            ]
            + [pl.BlockSpec(memory_space=pl.ANY) for _ in blocks],
            out_specs=[pl.BlockSpec((tok, width), lambda j, s: (0, 0))] * group,
            scratch_shapes=[
                pltpu.VMEM((planes, depth, width), jnp.bfloat16),
                pltpu.SemaphoreType.DMA((planes,)),
            ],
        ),
        compiler_params=pltpu.CompilerParams(
            dimension_semantics=("arbitrary",), vmem_limit_bytes=VMEM_LIMIT
        ),
        cost_estimate=pl.CostEstimate(
            flops=2 * tok * group * planes * depth * width,
            transcendentals=0,
            bytes_accessed=planes * depth * width * 2 + tok * group * planes * depth * 2,
        ),
        name="project",
    )(scalars, *pieces, *blocks)


def per_device(latent, w_kv, queries, w_out):
    planes, group, cols = lax.axis_size("grp"), lax.axis_size("mem"), lax.axis_size("col")
    grp, mem, col = lax.axis_index("grp"), lax.axis_index("mem"), lax.axis_index("col")
    per_col = queries.shape[1] // HEAD
    run = w_out.shape[0] // HEAD
    turns = per_col // (group * run)
    place = jnp.stack([grp, mem, col]).astype(jnp.int32)
    shifts = range(group)

    def swap(x, m):
        return lax.ppermute(x, "mem", [(p, p ^ m) for p in range(group)])

    def gather(x):
        return [x] + [swap(x, m) for m in range(1, group)]

    def exchange(xs):
        return [xs[0]] + [swap(xs[m], m) for m in range(1, group)]

    def up(x, k):
        return lax.ppermute(x, "grp", [(z, z + k) for z in range(planes - k)])

    def across(x, s):
        return lax.ppermute(x, "col", [((c + s) % cols, c) for c in range(cols)])

    def plane_swap(x, k, senders=None):
        senders = range(planes) if senders is None else senders
        return lax.ppermute(x, "grp", [(z, z ^ k) for z in senders])

    far_shift, half = planes - 1, planes // 2
    near = [z for z in range(planes) if abs(z - (z ^ far_shift)) == 1]
    far = [z for z in range(planes) if z not in near]
    is_near = functools.reduce(jnp.logical_or, [grp == z for z in near]).astype(jnp.int32)

    def relay(x):
        last = far_shift ^ half
        return plane_swap(x, last, [z ^ last for z in far])

    width = w_out.shape[1] // group
    first_width = -(-width // (2 * HEAD)) * HEAD
    spans = [(0, first_width), (first_width, width - first_width)]

    def by_turn(n):
        return [(m, n, [(t * group * n, n) for t in range(turns)]) for m in shifts]

    takes = [
        by_turn(run * 2 * HEAD),
        [(m, width, [span]) for span in spans for m in shifts],
        by_turn(run * HEAD),
    ]
    blocks = cut(place, [w_kv, w_out, queries], takes)
    w_mine = exchange(blocks[:group])
    lower = [up(latent, k) for k in range(planes - 1, 0, -1)]
    own = gather(latent)
    w_first = exchange(blocks[group : 2 * group])

    w_mine = jnp.stack(w_mine)
    w_all = [w_mine] + [plane_swap(w_mine, k) for k in range(1, planes)]

    middle_shifts = [half, *(k for k in range(1, far_shift) if k != half)]

    def spread(x):
        x = jnp.concatenate(x)
        return [x] + [plane_swap(x, k) for k in middle_shifts] + [plane_swap(x, far_shift, near)]

    out_first = spread(w_first)
    q_send, lower, _ = lax.optimization_barrier((blocks[3 * group :], lower, w_first[1:]))
    below = gather(jnp.concatenate(lower))
    my_queries = exchange(q_send)
    w_send, _ = lax.optimization_barrier((blocks[2 * group : 3 * group], my_queries))
    w_second = exchange(w_send)

    owns = [own] + [[across(x, s) for x in own] for s in range(1, cols)]
    belows = [below] + [[across(x, s) for x in below] for s in range(1, cols)]

    calls = [(t, t * run, run) for t in range(turns - 1)]
    calls += [((turns - 1), (turns - 1) * run + i, 1) for i in range(run)]
    results = [[] for _ in range(turns)]
    done = []
    for turn, first_head, heads in calls:
        i = len(done)
        done.append(attention(place, my_queries, owns, belows, w_all, first_head, heads))
        results[turn].append(gather(done[-1]))
        if i == 0:
            w_second, _ = lax.optimization_barrier((w_second, done[0]))
            out_second = spread(w_second)
    middle, _ = lax.optimization_barrier((out_first[1], done[max(len(done) - 2, 0)]))
    first_far = relay(middle)
    middle, _ = lax.optimization_barrier((out_second[1], done[-1]))
    second_far = relay(middle)

    sets, meets = [], []
    for turn in range(turns):
        for s in range(cols):
            some = [[x if s == 0 else across(x, s) for x in part] for part in results[turn]]
            sets.append([part[m] for m in shifts for part in some])
            meets.append((((col + s) % cols) * turns + turn) ^ grp)
    scalars = jnp.stack([*meets, mem, is_near]).astype(jnp.int32)

    def in_order(out, last):
        by_shift = {0: out[0], half: out[1], far_shift: out[-1]}
        by_shift.update(zip(middle_shifts[1:], out[2:-1]))
        return [by_shift[k] for k in range(planes)] + [last]

    mixed = []
    for out, last in ((out_first, first_far), (out_second, second_far)):
        columns = project(scalars, sets, in_order(out, last), group)
        got = exchange(columns)
        stack = jnp.stack(got)
        mixed.append([lax.dynamic_index_in_dim(stack, mem ^ p, 0, False) for p in shifts])
    return jnp.concatenate([part[p] for p in shifts for part in mixed], axis=1)


def solution(mesh):
    rows, cols = mesh.devices.shape
    group = 4
    fine = Mesh(mesh.devices.reshape(rows // group, group, cols), ("grp", "mem", "col"))
    spec = P(("grp", "mem"), "col")

    return jax.shard_map(per_device, mesh=fine, in_specs=(spec,) * 4, out_specs=spec, check_vma=False)
```

```python
import functools
import math

import jax
import jax.numpy as jnp
from jax import lax
from jax.experimental import pallas as pl
from jax.experimental.pallas import tpu as pltpu
from jax.sharding import Mesh, PartitionSpec as P


HEAD = 128
NEG_FILL = -1e30
VMEM_LIMIT = 56 * 1024 * 1024


def cut_kernel(place, *refs, takes):
    ins, outs = refs[: len(takes)], refs[len(takes) :]
    mem = place[1]
    at = 0
    for ref, take in zip(ins, takes):
        for m, stride, parts in take:
            done = 0
            for offset, width in parts:
                first = pl.multiple_of((mem ^ m) * stride + offset, HEAD)
                outs[at][:, done : done + width] = ref[:, pl.ds(first, width)]
                done += width
            at += 1


def cut(place, arrays, takes):
    flat = [(x, take) for x, some in zip(arrays, takes) for take in some]
    widths = [n for _, (_, stride, parts) in flat for n in (stride, *(v for p in parts for v in p))]
    if any(n % HEAD for n in widths):
        mem = place[1]
        return [
            jnp.concatenate(
                [lax.dynamic_slice_in_dim(x, (mem ^ m) * stride + o, n, 1) for o, n in parts], axis=1
            )
            for x, (m, stride, parts) in flat
        ]
    return pl.pallas_call(
        functools.partial(cut_kernel, takes=takes),
        out_shape=[
            jax.ShapeDtypeStruct((x.shape[0], sum(n for _, n in parts)), x.dtype)
            for x, (_, _, parts) in flat
        ],
        grid_spec=pltpu.PrefetchScalarGridSpec(
            num_scalar_prefetch=1,
            grid=(1,),
            in_specs=[pl.BlockSpec(x.shape, lambda i, s: (0, 0)) for x in arrays],
            out_specs=[
                pl.BlockSpec((x.shape[0], sum(n for _, n in parts)), lambda i, s: (0, 0))
                for x, (_, _, parts) in flat
            ],
        ),
        compiler_params=pltpu.CompilerParams(vmem_limit_bytes=VMEM_LIMIT),
        cost_estimate=pl.CostEstimate(
            flops=0, transcendentals=0, bytes_accessed=2 * sum(2 * x.size for x in arrays)
        ),
        name="cut",
    )(place, *arrays)


def attention_kernel(place, *refs, planes, group, cols, rate, parts):
    q_refs, refs = refs[:group], refs[group:]
    own, refs = refs[: cols * group], refs[cols * group :]
    before, refs = refs[: cols * group], refs[cols * group :]
    w_refs, refs = refs[:planes], refs[planes:]
    o_ref, q_sc, w_sc, kv_sc, m_sc, acc_sc = refs
    grp, mem, col = place[0], place[1], place[2]
    tok, features = own[0].shape
    plane = tok * group
    earlier = (planes - 1) * plane
    block = pl.program_id(1)
    size = o_ref.shape[0]
    rows = size // parts
    depth = w_refs[0].shape[1]

    def expand(sources, at, to):
        out = None
        for s in range(cols):
            w = w_sc[pl.ds(pl.multiple_of(((col + s) % cols) * features, features), features), :]
            term = jnp.dot(sources[s * group][at, :], w, preferred_element_type=jnp.float32)
            out = term if out is None else out + term
        kv_sc[to, :] = out.astype(kv_sc.dtype)

    @pl.when(block == 0)
    def _():
        for m in range(group):
            q_sc[pl.ds(pl.multiple_of((mem ^ m) * tok, tok), tok), :] = q_refs[m][...]
            for k in range(planes):
                first = ((grp ^ k) * group + (mem ^ m)) * depth
                w_sc[pl.ds(pl.multiple_of(first, depth), depth), :] = w_refs[k][m]
        for m in range(group):
            first = earlier + (mem ^ m) * tok
            expand(own[m:], pl.ds(0, tok), pl.ds(pl.multiple_of(first, tok), tok))

        def plane_before(t, _):
            for m in range(group):
                at = pl.ds(pl.multiple_of(t * tok, tok), tok)
                expand(before[m:], at, pl.ds(pl.multiple_of(t * plane + m * tok, tok), tok))
            return 0

        lax.fori_loop(planes - 1 - grp, planes - 1, plane_before, 0)

    m_sc[...] = jnp.full_like(m_sc, NEG_FILL)
    acc_sc[...] = jnp.zeros_like(acc_sc)
    base = pl.multiple_of(block * size, size)

    def step(first, width, query_at=None):
        keys = kv_sc[pl.ds(first, width), :HEAD]
        values = kv_sc[pl.ds(first, width), HEAD:]
        values = jnp.concatenate([values, jnp.ones_like(values)], axis=1)
        scores = []
        for u in range(parts):
            s = lax.dot_general(
                q_sc[pl.ds(base + u * rows, rows), :],
                keys,
                (((1,), (1,)), ((), ())),
                preferred_element_type=jnp.float32,
            )
            if query_at is not None:
                row = lax.broadcasted_iota(jnp.int32, s.shape, 0) + (query_at + u * rows)
                column = lax.broadcasted_iota(jnp.int32, s.shape, 1)
                s = jnp.where(column <= row, s, NEG_FILL)
            scores.append(s)
        for u in range(parts):
            at = slice(u * rows, (u + 1) * rows)
            old = m_sc[at]
            new = jnp.maximum(old, jnp.max(scores[u], axis=1, keepdims=True))
            m_sc[at] = new
            shifted = scores[u] - jnp.tile(new, (1, width // HEAD))
            weights = jnp.exp2(shifted * rate).astype(jnp.bfloat16)
            again = jnp.exp2((old - new) * rate)
            acc_sc[at] = acc_sc[at] * jnp.concatenate([again, again], axis=1) + jnp.dot(
                weights, values, preferred_element_type=jnp.float32
            )

    def plane_step(t, _):
        step(pl.multiple_of(t * plane, plane), plane)
        return 0

    for b in range(plane // size):

        @pl.when(block == b)
        def _():
            step(earlier, (b + 1) * size, b * size)

    lax.fori_loop(planes - 1 - grp, planes - 1, plane_step, 0)
    o_ref[...] = (acc_sc[:, :HEAD] / acc_sc[:, HEAD:]).astype(o_ref.dtype)


def attention(place, queries, own, before, w, first_head, heads):
    planes, group, cols = len(w), len(queries), len(own)
    tok, features = own[0][0].shape
    plane = tok * group
    total = planes * plane
    size = plane // 2
    fixed = lambda h, j, s: (0, 0)
    whole = [pl.BlockSpec(x.shape, fixed, pipeline_mode=pl.Buffered(1)) for x in own[0] * cols]
    whole += [pl.BlockSpec(x.shape, fixed, pipeline_mode=pl.Buffered(1)) for x in before[0] * cols]
    return pl.pallas_call(
        functools.partial(
            attention_kernel,
            planes=planes,
            group=group,
            cols=cols,
            rate=HEAD**-0.5 * math.log2(math.e),
            parts=2,
        ),
        out_shape=jax.ShapeDtypeStruct((plane, heads * HEAD), jnp.bfloat16),
        grid_spec=pltpu.PrefetchScalarGridSpec(
            num_scalar_prefetch=1,
            grid=(heads, plane // size),
            in_specs=[pl.BlockSpec((tok, HEAD), lambda h, j, s: (0, h + first_head)) for _ in queries]
            + whole
            + [
                pl.BlockSpec((*x.shape[:2], 2 * HEAD), lambda h, j, s: (0, 0, h + first_head)) for x in w
            ],
            out_specs=pl.BlockSpec((size, HEAD), lambda h, j, s: (j, h)),
            scratch_shapes=[
                pltpu.VMEM((plane, HEAD), jnp.bfloat16),
                pltpu.VMEM((features * cols, 2 * HEAD), jnp.bfloat16),
                pltpu.VMEM((total, 2 * HEAD), jnp.bfloat16),
                pltpu.VMEM((size, HEAD), jnp.float32),
                pltpu.VMEM((size, 2 * HEAD), jnp.float32),
            ],
        ),
        compiler_params=pltpu.CompilerParams(
            dimension_semantics=("arbitrary", "arbitrary"), vmem_limit_bytes=VMEM_LIMIT
        ),
        cost_estimate=pl.CostEstimate(
            flops=heads * plane * total * HEAD * 6,
            transcendentals=heads * plane * total,
            bytes_accessed=total * features * cols * 2,
        ),
        name="attention",
    )(place, *queries, *(x for some in own for x in some), *(x for some in before for x in some), *w)


def project_kernel(scalars, *refs, counts, group, planes):
    a_refs, refs = refs[: sum(counts)], refs[sum(counts) :]
    b_refs, refs = refs[: planes + 1], refs[planes + 1 :]
    outs, (b_sc, sems) = refs[:group], refs[group:]
    step = pl.program_id(0)
    near = scalars[len(counts) + 1] == 1

    @pl.when(step == 0)
    def _():
        copies = [pltpu.make_async_copy(b_refs[k], b_sc.at[k], sems.at[k]) for k in range(planes - 1)]
        for copy in copies:
            copy.start()
        for which, source in ((near, b_refs[planes - 1]), (jnp.logical_not(near), b_refs[planes])):

            @pl.when(which)
            def _():
                copy = pltpu.make_async_copy(source, b_sc.at[planes - 1], sems.at[planes - 1])
                copy.start()
                copy.wait()

        for copy in copies:
            copy.wait()

    out, at = None, 0
    for x, count in enumerate(counts):
        heads = [a_refs[at + i][...] for i in range(count)]
        a = heads[0] if count == 1 else jnp.concatenate(heads, axis=1)
        term = jnp.dot(a, b_sc[scalars[x]], preferred_element_type=jnp.float32)
        out = term if out is None else out + term
        at += count
    for m in range(group):

        @pl.when(step == m)
        def _():
            outs[m][...] = out.astype(outs[m].dtype)


def project(scalars, sets, blocks, group):
    pieces = [x for some in sets for x in some]
    planes = len(blocks) - 1
    tok = pieces[0].shape[0] // group
    depth, width = blocks[0].shape
    count = len(sets)
    return pl.pallas_call(
        functools.partial(
            project_kernel, counts=[len(some) for some in sets], group=group, planes=planes
        ),
        out_shape=[jax.ShapeDtypeStruct((tok, width), jnp.bfloat16)] * group,
        grid_spec=pltpu.PrefetchScalarGridSpec(
            num_scalar_prefetch=1,
            grid=(group,),
            in_specs=[
                pl.BlockSpec((tok, x.shape[1]), lambda j, s: (s[count] ^ j, 0)) for x in pieces
            ]
            + [pl.BlockSpec(memory_space=pl.ANY) for _ in blocks],
            out_specs=[pl.BlockSpec((tok, width), lambda j, s: (0, 0))] * group,
            scratch_shapes=[
                pltpu.VMEM((planes, depth, width), jnp.bfloat16),
                pltpu.SemaphoreType.DMA((planes,)),
            ],
        ),
        compiler_params=pltpu.CompilerParams(
            dimension_semantics=("arbitrary",), vmem_limit_bytes=VMEM_LIMIT
        ),
        cost_estimate=pl.CostEstimate(
            flops=2 * tok * group * planes * depth * width,
            transcendentals=0,
            bytes_accessed=planes * depth * width * 2 + tok * group * planes * depth * 2,
        ),
        name="project",
    )(scalars, *pieces, *blocks)


def per_device(latent, w_kv, queries, w_out):
    planes, group, cols = lax.axis_size("grp"), lax.axis_size("mem"), lax.axis_size("col")
    grp, mem, col = lax.axis_index("grp"), lax.axis_index("mem"), lax.axis_index("col")
    per_col = queries.shape[1] // HEAD
    run = w_out.shape[0] // HEAD
    turns = per_col // (group * run)
    place = jnp.stack([grp, mem, col]).astype(jnp.int32)
    shifts = range(group)

    def swap(x, m):
        return lax.ppermute(x, "mem", [(p, p ^ m) for p in range(group)])

    def gather(x):
        return [x] + [swap(x, m) for m in range(1, group)]

    def exchange(xs):
        return [xs[0]] + [swap(xs[m], m) for m in range(1, group)]

    def up(x, k):
        return lax.ppermute(x, "grp", [(z, z + k) for z in range(planes - k)])

    def across(x, s):
        return lax.ppermute(x, "col", [((c + s) % cols, c) for c in range(cols)])

    def plane_swap(x, k, senders=None):
        senders = range(planes) if senders is None else senders
        return lax.ppermute(x, "grp", [(z, z ^ k) for z in senders])

    far_shift, half = planes - 1, planes // 2
    near = [z for z in range(planes) if abs(z - (z ^ far_shift)) == 1]
    far = [z for z in range(planes) if z not in near]
    is_near = functools.reduce(jnp.logical_or, [grp == z for z in near]).astype(jnp.int32)

    def relay(x):
        last = far_shift ^ half
        return plane_swap(x, last, [z ^ last for z in far])

    width = w_out.shape[1] // group
    first_width = -(-width // (2 * HEAD)) * HEAD
    spans = [(0, first_width), (first_width, width - first_width)]

    def by_turn(n):
        return [(m, n, [(t * group * n, n) for t in range(turns)]) for m in shifts]

    takes = [
        by_turn(run * 2 * HEAD),
        [(m, width, [span]) for span in spans for m in shifts],
        by_turn(run * HEAD),
    ]
    blocks = cut(place, [w_kv, w_out, queries], takes)
    w_mine = exchange(blocks[:group])
    lower = [up(latent, k) for k in range(planes - 1, 0, -1)]
    own = gather(latent)
    w_first = exchange(blocks[group : 2 * group])

    w_mine = jnp.stack(w_mine)
    w_all = [w_mine] + [plane_swap(w_mine, k) for k in range(1, planes)]

    middle_shifts = [half, *(k for k in range(1, far_shift) if k != half)]

    def spread(x):
        x = jnp.concatenate(x)
        return [x] + [plane_swap(x, k) for k in middle_shifts] + [plane_swap(x, far_shift, near)]

    out_first = spread(w_first)
    below = gather(jnp.concatenate(lower))
    my_queries = exchange(blocks[3 * group :])
    w_second = exchange(blocks[2 * group : 3 * group])

    owns = [own] + [[across(x, s) for x in own] for s in range(1, cols)]
    belows = [below] + [[across(x, s) for x in below] for s in range(1, cols)]

    calls = [(t, t * run, run) for t in range(turns - 1)]
    calls += [((turns - 1), (turns - 1) * run + i, 1) for i in range(run)]
    results = [[] for _ in range(turns)]
    done = []
    for turn, first_head, heads in calls:
        i = len(done)
        done.append(attention(place, my_queries, owns, belows, w_all, first_head, heads))
        results[turn].append(gather(done[-1]))
        if i == 0:
            w_second, _ = lax.optimization_barrier((w_second, done[0]))
            out_second = spread(w_second)
    middle, _ = lax.optimization_barrier((out_first[1], done[max(len(done) - 2, 0)]))
    first_far = relay(middle)
    middle, _ = lax.optimization_barrier((out_second[1], done[-1]))
    second_far = relay(middle)

    sets, meets = [], []
    for turn in range(turns):
        for s in range(cols):
            some = [[x if s == 0 else across(x, s) for x in part] for part in results[turn]]
            sets.append([part[m] for m in shifts for part in some])
            meets.append((((col + s) % cols) * turns + turn) ^ grp)
    scalars = jnp.stack([*meets, mem, is_near]).astype(jnp.int32)

    def in_order(out, last):
        by_shift = {0: out[0], half: out[1], far_shift: out[-1]}
        by_shift.update(zip(middle_shifts[1:], out[2:-1]))
        return [by_shift[k] for k in range(planes)] + [last]

    mixed = []
    for out, last in ((out_first, first_far), (out_second, second_far)):
        columns = project(scalars, sets, in_order(out, last), group)
        got = exchange(columns)
        stack = jnp.stack(got)
        mixed.append([lax.dynamic_index_in_dim(stack, mem ^ p, 0, False) for p in shifts])
    return jnp.concatenate([part[p] for p in shifts for part in mixed], axis=1)


def solution(mesh):
    rows, cols = mesh.devices.shape
    group = 4
    fine = Mesh(mesh.devices.reshape(rows // group, group, cols), ("grp", "mem", "col"))
    spec = P(("grp", "mem"), "col")

    return jax.shard_map(per_device, mesh=fine, in_specs=(spec,) * 4, out_specs=spec, check_vma=False)
```

```python
import functools
import math

import jax
import jax.numpy as jnp
from jax import lax
from jax.experimental import pallas as pl
from jax.experimental.pallas import tpu as pltpu
from jax.sharding import Mesh, PartitionSpec as P


HEAD = 128
NEG_FILL = -1e30
VMEM_LIMIT = 56 * 1024 * 1024


def cut_kernel(place, *refs, takes):
    ins, outs = refs[: len(takes)], refs[len(takes) :]
    mem = place[1]
    at = 0
    for ref, take in zip(ins, takes):
        for m, stride, parts in take:
            done = 0
            for offset, width in parts:
                first = pl.multiple_of((mem ^ m) * stride + offset, HEAD)
                outs[at][:, done : done + width] = ref[:, pl.ds(first, width)]
                done += width
            at += 1


def cut(place, arrays, takes):
    flat = [(x, take) for x, some in zip(arrays, takes) for take in some]
    widths = [n for _, (_, stride, parts) in flat for n in (stride, *(v for p in parts for v in p))]
    if any(n % HEAD for n in widths):
        mem = place[1]
        return [
            jnp.concatenate(
                [lax.dynamic_slice_in_dim(x, (mem ^ m) * stride + o, n, 1) for o, n in parts], axis=1
            )
            for x, (m, stride, parts) in flat
        ]
    return pl.pallas_call(
        functools.partial(cut_kernel, takes=takes),
        out_shape=[
            jax.ShapeDtypeStruct((x.shape[0], sum(n for _, n in parts)), x.dtype)
            for x, (_, _, parts) in flat
        ],
        grid_spec=pltpu.PrefetchScalarGridSpec(
            num_scalar_prefetch=1,
            grid=(1,),
            in_specs=[pl.BlockSpec(x.shape, lambda i, s: (0, 0)) for x in arrays],
            out_specs=[
                pl.BlockSpec((x.shape[0], sum(n for _, n in parts)), lambda i, s: (0, 0))
                for x, (_, _, parts) in flat
            ],
        ),
        compiler_params=pltpu.CompilerParams(vmem_limit_bytes=VMEM_LIMIT),
        cost_estimate=pl.CostEstimate(
            flops=0, transcendentals=0, bytes_accessed=2 * sum(2 * x.size for x in arrays)
        ),
        name="cut",
    )(place, *arrays)


def attention_kernel(place, *refs, planes, group, cols, rate, parts):
    q_refs, refs = refs[:group], refs[group:]
    own, refs = refs[: cols * group], refs[cols * group :]
    before, refs = refs[: cols * group], refs[cols * group :]
    w_refs, refs = refs[:planes], refs[planes:]
    o_ref, q_sc, w_sc, kv_sc, m_sc, acc_sc, before_sc, sems = refs
    grp, mem, col = place[0], place[1], place[2]
    tok, features = own[0].shape
    plane = tok * group
    earlier = (planes - 1) * plane
    block = pl.program_id(1)
    size = o_ref.shape[0]
    rows = size // parts
    depth = w_refs[0].shape[1]

    first_step = jnp.logical_and(pl.program_id(0) == 0, block == 0)
    copies = [
        pltpu.make_async_copy(before[i], before_sc.at[i], sems.at[i]) for i in range(cols * group)
    ]

    @pl.when(first_step)
    def _():
        for copy in copies:
            copy.start()

    def expand(load, to):
        out = None
        for s in range(cols):
            w = w_sc[pl.ds(pl.multiple_of(((col + s) % cols) * features, features), features), :]
            term = jnp.dot(load(s), w, preferred_element_type=jnp.float32)
            out = term if out is None else out + term
        kv_sc[to, :] = out.astype(kv_sc.dtype)

    @pl.when(block == 0)
    def _():
        for m in range(group):
            q_sc[pl.ds(pl.multiple_of((mem ^ m) * tok, tok), tok), :] = q_refs[m][...]
            for k in range(planes):
                first = ((grp ^ k) * group + (mem ^ m)) * depth
                w_sc[pl.ds(pl.multiple_of(first, depth), depth), :] = w_refs[k][m]
        for m in range(group):
            first = earlier + (mem ^ m) * tok
            expand(lambda s: own[s * group + m][...], pl.ds(pl.multiple_of(first, tok), tok))

    m_sc[...] = jnp.full_like(m_sc, NEG_FILL)
    acc_sc[...] = jnp.zeros_like(acc_sc)
    base = pl.multiple_of(block * size, size)

    def step(first, width, query_at=None):
        keys = kv_sc[pl.ds(first, width), :HEAD]
        values = kv_sc[pl.ds(first, width), HEAD:]
        values = jnp.concatenate([values, jnp.ones_like(values)], axis=1)
        scores = []
        for u in range(parts):
            s = lax.dot_general(
                q_sc[pl.ds(base + u * rows, rows), :],
                keys,
                (((1,), (1,)), ((), ())),
                preferred_element_type=jnp.float32,
            )
            if query_at is not None:
                row = lax.broadcasted_iota(jnp.int32, s.shape, 0) + (query_at + u * rows)
                column = lax.broadcasted_iota(jnp.int32, s.shape, 1)
                s = jnp.where(column <= row, s, NEG_FILL)
            scores.append(s)
        for u in range(parts):
            at = slice(u * rows, (u + 1) * rows)
            old = m_sc[at]
            new = jnp.maximum(old, jnp.max(scores[u], axis=1, keepdims=True))
            m_sc[at] = new
            shifted = scores[u] - jnp.tile(new, (1, width // HEAD))
            weights = jnp.exp2(shifted * rate).astype(jnp.bfloat16)
            again = jnp.exp2((old - new) * rate)
            acc_sc[at] = acc_sc[at] * jnp.concatenate([again, again], axis=1) + jnp.dot(
                weights, values, preferred_element_type=jnp.float32
            )

    def plane_step(t, _):
        step(pl.multiple_of(t * plane, plane), plane)
        return 0

    for b in range(plane // size):

        @pl.when(block == b)
        def _():
            step(earlier, (b + 1) * size, b * size)

    @pl.when(first_step)
    def _():
        for copy in copies:
            copy.wait()

    @pl.when(block == 0)
    def _():
        def plane_before(t, _):
            at = pl.ds(pl.multiple_of(t * tok, tok), tok)
            for m in range(group):
                expand(
                    lambda s: before_sc[s * group + m, at, :],
                    pl.ds(pl.multiple_of(t * plane + m * tok, tok), tok),
                )
            return 0

        lax.fori_loop(planes - 1 - grp, planes - 1, plane_before, 0)

    lax.fori_loop(planes - 1 - grp, planes - 1, plane_step, 0)
    o_ref[...] = (acc_sc[:, :HEAD] / acc_sc[:, HEAD:]).astype(o_ref.dtype)


def attention(place, queries, own, before, w, first_query, first_head, heads):
    planes, group, cols = len(w), len(queries), len(own)
    tok, features = own[0][0].shape
    plane = tok * group
    total = planes * plane
    size = plane
    fixed = lambda h, j, s: (0, 0)
    whole = [pl.BlockSpec(x.shape, fixed, pipeline_mode=pl.Buffered(1)) for x in own[0] * cols]
    whole += [pl.BlockSpec(memory_space=pl.ANY) for _ in before[0] * cols]
    return pl.pallas_call(
        functools.partial(
            attention_kernel,
            planes=planes,
            group=group,
            cols=cols,
            rate=HEAD**-0.5 * math.log2(math.e),
            parts=2,
        ),
        out_shape=jax.ShapeDtypeStruct((plane, heads * HEAD), jnp.bfloat16),
        grid_spec=pltpu.PrefetchScalarGridSpec(
            num_scalar_prefetch=1,
            grid=(heads, plane // size),
            in_specs=[pl.BlockSpec((tok, HEAD), lambda h, j, s: (0, h + first_query)) for _ in queries]
            + whole
            + [
                pl.BlockSpec((*x.shape[:2], 2 * HEAD), lambda h, j, s: (0, 0, h + first_head)) for x in w
            ],
            out_specs=pl.BlockSpec((size, HEAD), lambda h, j, s: (j, h)),
            scratch_shapes=[
                pltpu.VMEM((plane, HEAD), jnp.bfloat16),
                pltpu.VMEM((features * cols, 2 * HEAD), jnp.bfloat16),
                pltpu.VMEM((total, 2 * HEAD), jnp.bfloat16),
                pltpu.VMEM((size, HEAD), jnp.float32),
                pltpu.VMEM((size, 2 * HEAD), jnp.float32),
                pltpu.VMEM((cols * group, *before[0][0].shape), jnp.bfloat16),
                pltpu.SemaphoreType.DMA((cols * group,)),
            ],
        ),
        compiler_params=pltpu.CompilerParams(
            dimension_semantics=("arbitrary", "arbitrary"), vmem_limit_bytes=VMEM_LIMIT
        ),
        cost_estimate=pl.CostEstimate(
            flops=heads * plane * total * HEAD * 6,
            transcendentals=heads * plane * total,
            bytes_accessed=total * features * cols * 2,
        ),
        name="attention",
    )(place, *queries, *(x for some in own for x in some), *(x for some in before for x in some), *w)


def project_kernel(scalars, *refs, counts, group, planes):
    a_refs, refs = refs[: sum(counts)], refs[sum(counts) :]
    b_refs, refs = refs[: planes + 1], refs[planes + 1 :]
    outs, (b_sc, sems) = refs[:group], refs[group:]
    step = pl.program_id(0)
    near = scalars[len(counts) + 1] == 1

    @pl.when(step == 0)
    def _():
        copies = [pltpu.make_async_copy(b_refs[k], b_sc.at[k], sems.at[k]) for k in range(planes - 1)]
        for copy in copies:
            copy.start()
        for which, source in ((near, b_refs[planes - 1]), (jnp.logical_not(near), b_refs[planes])):

            @pl.when(which)
            def _():
                copy = pltpu.make_async_copy(source, b_sc.at[planes - 1], sems.at[planes - 1])
                copy.start()
                copy.wait()

        for copy in copies:
            copy.wait()

    out, at = None, 0
    for x, count in enumerate(counts):
        heads = [a_refs[at + i][...] for i in range(count)]
        a = heads[0] if count == 1 else jnp.concatenate(heads, axis=1)
        term = jnp.dot(a, b_sc[scalars[x]], preferred_element_type=jnp.float32)
        out = term if out is None else out + term
        at += count
    for m in range(group):

        @pl.when(step == m)
        def _():
            outs[m][...] = out.astype(outs[m].dtype)


def project(scalars, sets, blocks, group):
    pieces = [x for some in sets for x in some]
    planes = len(blocks) - 1
    tok = pieces[0].shape[0] // group
    depth, width = blocks[0].shape
    count = len(sets)
    return pl.pallas_call(
        functools.partial(
            project_kernel, counts=[len(some) for some in sets], group=group, planes=planes
        ),
        out_shape=[jax.ShapeDtypeStruct((tok, width), jnp.bfloat16)] * group,
        grid_spec=pltpu.PrefetchScalarGridSpec(
            num_scalar_prefetch=1,
            grid=(group,),
            in_specs=[
                pl.BlockSpec((tok, x.shape[1]), lambda j, s: (s[count] ^ j, 0)) for x in pieces
            ]
            + [pl.BlockSpec(memory_space=pl.ANY) for _ in blocks],
            out_specs=[pl.BlockSpec((tok, width), lambda j, s: (0, 0))] * group,
            scratch_shapes=[
                pltpu.VMEM((planes, depth, width), jnp.bfloat16),
                pltpu.SemaphoreType.DMA((planes,)),
            ],
        ),
        compiler_params=pltpu.CompilerParams(
            dimension_semantics=("arbitrary",), vmem_limit_bytes=VMEM_LIMIT
        ),
        cost_estimate=pl.CostEstimate(
            flops=2 * tok * group * planes * depth * width,
            transcendentals=0,
            bytes_accessed=planes * depth * width * 2 + tok * group * planes * depth * 2,
        ),
        name="project",
    )(scalars, *pieces, *blocks)


def per_device(latent, w_kv, queries, w_out):
    planes, group, cols = lax.axis_size("grp"), lax.axis_size("mem"), lax.axis_size("col")
    grp, mem, col = lax.axis_index("grp"), lax.axis_index("mem"), lax.axis_index("col")
    per_col = queries.shape[1] // HEAD
    run = w_out.shape[0] // HEAD
    turns = per_col // (group * run)
    place = jnp.stack([grp, mem, col]).astype(jnp.int32)
    shifts = range(group)

    def swap(x, m):
        return lax.ppermute(x, "mem", [(p, p ^ m) for p in range(group)])

    def gather(x):
        return [x] + [swap(x, m) for m in range(1, group)]

    def exchange(xs):
        return [xs[0]] + [swap(xs[m], m) for m in range(1, group)]

    def up(x, k):
        return lax.ppermute(x, "grp", [(z, z + k) for z in range(planes - k)])

    def across(x, s):
        return lax.ppermute(x, "col", [((c + s) % cols, c) for c in range(cols)])

    def plane_swap(x, k, senders=None):
        senders = range(planes) if senders is None else senders
        return lax.ppermute(x, "grp", [(z, z ^ k) for z in senders])

    far_shift, half = planes - 1, planes // 2
    near = [z for z in range(planes) if abs(z - (z ^ far_shift)) == 1]
    far = [z for z in range(planes) if z not in near]
    is_near = functools.reduce(jnp.logical_or, [grp == z for z in near]).astype(jnp.int32)

    def relay(x):
        last = far_shift ^ half
        return plane_swap(x, last, [z ^ last for z in far])

    width = w_out.shape[1] // group
    first_width = -(-width // (2 * HEAD)) * HEAD
    spans = [(0, first_width), (first_width, width - first_width)]

    def by_turn(n):
        return [(m, n, [(t * group * n, n) for t in range(turns)]) for m in shifts]

    takes = [
        by_turn(run * 2 * HEAD),
        [(m, width, [span]) for span in spans for m in shifts],
        [(m, run * HEAD, [(t * group * run * HEAD, run * HEAD)]) for t in range(turns) for m in shifts],
    ]
    blocks = cut(place, [w_kv, w_out, queries], takes)
    w_mine = exchange(blocks[:group])
    lower = [up(latent, k) for k in range(planes - 1, 0, -1)]
    own = gather(latent)
    w_first = exchange(blocks[group : 2 * group])

    w_mine = jnp.stack(w_mine)
    w_all = [w_mine] + [plane_swap(w_mine, k) for k in range(1, planes)]

    middle_shifts = [half, *(k for k in range(1, far_shift) if k != half)]

    def spread(x):
        x = jnp.concatenate(x)
        return [x] + [plane_swap(x, k) for k in middle_shifts] + [plane_swap(x, far_shift, near)]

    out_first = spread(w_first)
    below = gather(jnp.concatenate(lower))
    my_queries = [exchange(blocks[(3 + t) * group : (4 + t) * group]) for t in range(turns)]
    w_second = exchange(blocks[2 * group : 3 * group])

    owns = [own] + [[across(x, s) for x in own] for s in range(1, cols)]
    belows = [below] + [[across(x, s) for x in below] for s in range(1, cols)]

    calls = [(t, t * run, run) for t in range(turns - 1)]
    calls += [((turns - 1), (turns - 1) * run + i, 1) for i in range(run)]
    results = [[] for _ in range(turns)]
    done = []
    for turn, first_head, heads in calls:
        i = len(done)
        done.append(attention(place, my_queries[turn], owns, belows, w_all, first_head - turn * run, first_head, heads))
        results[turn].append(gather(done[-1]))
        if i == 0:
            w_second, _ = lax.optimization_barrier((w_second, done[0]))
            out_second = spread(w_second)
    middle, _ = lax.optimization_barrier((out_first[1], done[0]))
    first_far = relay(middle)
    middle, _ = lax.optimization_barrier((out_second[1], done[-1]))
    second_far = relay(middle)

    sets, meets = [], []
    for turn in range(turns):
        for s in range(cols):
            some = [[x if s == 0 else across(x, s) for x in part] for part in results[turn]]
            sets.append([part[m] for m in shifts for part in some])
            meets.append((((col + s) % cols) * turns + turn) ^ grp)
    scalars = jnp.stack([*meets, mem, is_near]).astype(jnp.int32)

    def in_order(out, last):
        by_shift = {0: out[0], half: out[1], far_shift: out[-1]}
        by_shift.update(zip(middle_shifts[1:], out[2:-1]))
        return [by_shift[k] for k in range(planes)] + [last]

    mixed = []
    for out, last in ((out_first, first_far), (out_second, second_far)):
        columns = project(scalars, sets, in_order(out, last), group)
        got = exchange(columns)
        stack = jnp.stack(got)
        mixed.append([lax.dynamic_index_in_dim(stack, mem ^ p, 0, False) for p in shifts])
    return jnp.concatenate([part[p] for p in shifts for part in mixed], axis=1)


def solution(mesh):
    rows, cols = mesh.devices.shape
    group = 4
    fine = Mesh(mesh.devices.reshape(rows // group, group, cols), ("grp", "mem", "col"))
    spec = P(("grp", "mem"), "col")

    return jax.shard_map(per_device, mesh=fine, in_specs=(spec,) * 4, out_specs=spec, check_vma=False)
```

```python
import functools
import math

import jax
import jax.numpy as jnp
from jax import lax
from jax.experimental import pallas as pl
from jax.experimental.pallas import tpu as pltpu
from jax.sharding import Mesh, PartitionSpec as P


HEAD = 128
NEG_FILL = -1e30
VMEM_LIMIT = 56 * 1024 * 1024


def cut_kernel(place, *refs, takes):
    ins, outs = refs[: len(takes)], refs[len(takes) :]
    mem = place[1]
    at = 0
    for ref, take in zip(ins, takes):
        for m, stride, parts in take:
            done = 0
            for offset, width in parts:
                first = pl.multiple_of((mem ^ m) * stride + offset, HEAD)
                outs[at][:, done : done + width] = ref[:, pl.ds(first, width)]
                done += width
            at += 1


def cut(place, arrays, takes):
    flat = [(x, take) for x, some in zip(arrays, takes) for take in some]
    widths = [n for _, (_, stride, parts) in flat for n in (stride, *(v for p in parts for v in p))]
    if any(n % HEAD for n in widths):
        mem = place[1]
        return [
            jnp.concatenate(
                [lax.dynamic_slice_in_dim(x, (mem ^ m) * stride + o, n, 1) for o, n in parts], axis=1
            )
            for x, (m, stride, parts) in flat
        ]
    return pl.pallas_call(
        functools.partial(cut_kernel, takes=takes),
        out_shape=[
            jax.ShapeDtypeStruct((x.shape[0], sum(n for _, n in parts)), x.dtype)
            for x, (_, _, parts) in flat
        ],
        grid_spec=pltpu.PrefetchScalarGridSpec(
            num_scalar_prefetch=1,
            grid=(1,),
            in_specs=[pl.BlockSpec(x.shape, lambda i, s: (0, 0)) for x in arrays],
            out_specs=[
                pl.BlockSpec((x.shape[0], sum(n for _, n in parts)), lambda i, s: (0, 0))
                for x, (_, _, parts) in flat
            ],
        ),
        compiler_params=pltpu.CompilerParams(vmem_limit_bytes=VMEM_LIMIT),
        cost_estimate=pl.CostEstimate(
            flops=0, transcendentals=0, bytes_accessed=2 * sum(2 * x.size for x in arrays)
        ),
        name="cut",
    )(place, *arrays)


def attention_kernel(place, *refs, planes, group, cols, layout, rate, parts):
    q_refs, refs = refs[:group], refs[group:]
    own, refs = refs[: cols * group], refs[cols * group :]
    before, refs = refs[: cols * len(layout)], refs[cols * len(layout) :]
    w_refs, refs = refs[:planes], refs[planes:]
    o_ref, q_sc, w_sc, kv_sc, m_sc, acc_sc, before_sc, sems = refs
    grp, mem, col = place[0], place[1], place[2]
    tok, features = own[0].shape
    plane = tok * group
    earlier = (planes - 1) * plane
    block = pl.program_id(1)
    size = o_ref.shape[0]
    rows = size // parts
    depth = w_refs[0].shape[1]

    first_step = jnp.logical_and(pl.program_id(0) == 0, block == 0)
    copies = []
    for s in range(cols):
        for i, (m, start, count) in enumerate(layout):
            at = s * len(layout) + i
            target = before_sc.at[s * group + m, pl.ds(start, count), :]
            copies.append(pltpu.make_async_copy(before[at], target, sems.at[at]))

    @pl.when(first_step)
    def _():
        for copy in copies:
            copy.start()

    def expand(load, to):
        out = None
        for s in range(cols):
            w = w_sc[pl.ds(pl.multiple_of(((col + s) % cols) * features, features), features), :]
            term = jnp.dot(load(s), w, preferred_element_type=jnp.float32)
            out = term if out is None else out + term
        kv_sc[to, :] = out.astype(kv_sc.dtype)

    @pl.when(block == 0)
    def _():
        for m in range(group):
            q_sc[pl.ds(pl.multiple_of((mem ^ m) * tok, tok), tok), :] = q_refs[m][...]
            for k in range(planes):
                first = ((grp ^ k) * group + (mem ^ m)) * depth
                w_sc[pl.ds(pl.multiple_of(first, depth), depth), :] = w_refs[k][m]
        for m in range(group):
            first = earlier + (mem ^ m) * tok
            expand(lambda s: own[s * group + m][...], pl.ds(pl.multiple_of(first, tok), tok))

    m_sc[...] = jnp.full_like(m_sc, NEG_FILL)
    acc_sc[...] = jnp.zeros_like(acc_sc)
    base = pl.multiple_of(block * size, size)

    def step(first, width, query_at=None):
        keys = kv_sc[pl.ds(first, width), :HEAD]
        values = kv_sc[pl.ds(first, width), HEAD:]
        values = jnp.concatenate([values, jnp.ones_like(values)], axis=1)
        scores = []
        for u in range(parts):
            s = lax.dot_general(
                q_sc[pl.ds(base + u * rows, rows), :],
                keys,
                (((1,), (1,)), ((), ())),
                preferred_element_type=jnp.float32,
            )
            if query_at is not None:
                row = lax.broadcasted_iota(jnp.int32, s.shape, 0) + (query_at + u * rows)
                column = lax.broadcasted_iota(jnp.int32, s.shape, 1)
                s = jnp.where(column <= row, s, NEG_FILL)
            scores.append(s)
        for u in range(parts):
            at = slice(u * rows, (u + 1) * rows)
            old = m_sc[at]
            new = jnp.maximum(old, jnp.max(scores[u], axis=1, keepdims=True))
            m_sc[at] = new
            shifted = scores[u] - jnp.tile(new, (1, width // HEAD))
            weights = jnp.exp2(shifted * rate).astype(jnp.bfloat16)
            again = jnp.exp2((old - new) * rate)
            acc_sc[at] = acc_sc[at] * jnp.concatenate([again, again], axis=1) + jnp.dot(
                weights, values, preferred_element_type=jnp.float32
            )

    def plane_step(t, _):
        step(pl.multiple_of(t * plane, plane), plane)
        return 0

    for b in range(plane // size):

        @pl.when(block == b)
        def _():
            step(earlier, (b + 1) * size, b * size)

    @pl.when(first_step)
    def _():
        for copy in copies:
            copy.wait()

    @pl.when(block == 0)
    def _():
        def plane_before(t, _):
            at = pl.ds(pl.multiple_of(t * tok, tok), tok)
            for m in range(group):
                expand(
                    lambda s: before_sc[s * group + m, at, :],
                    pl.ds(pl.multiple_of(t * plane + m * tok, tok), tok),
                )
            return 0

        lax.fori_loop(planes - 1 - grp, planes - 1, plane_before, 0)

    lax.fori_loop(planes - 1 - grp, planes - 1, plane_step, 0)
    o_ref[...] = (acc_sc[:, :HEAD] / acc_sc[:, HEAD:]).astype(o_ref.dtype)


def attention(place, queries, own, before, layout, w, first_query, first_head, heads):
    planes, group, cols = len(w), len(queries), len(own)
    tok, features = own[0][0].shape
    plane = tok * group
    total = planes * plane
    size = plane
    fixed = lambda h, j, s: (0, 0)
    whole = [pl.BlockSpec(x.shape, fixed, pipeline_mode=pl.Buffered(1)) for x in own[0] * cols]
    whole += [pl.BlockSpec(memory_space=pl.ANY) for _ in before[0] * cols]
    return pl.pallas_call(
        functools.partial(
            attention_kernel,
            planes=planes,
            group=group,
            cols=cols,
            layout=layout,
            rate=HEAD**-0.5 * math.log2(math.e),
            parts=2,
        ),
        out_shape=jax.ShapeDtypeStruct((plane, heads * HEAD), jnp.bfloat16),
        grid_spec=pltpu.PrefetchScalarGridSpec(
            num_scalar_prefetch=1,
            grid=(heads, plane // size),
            in_specs=[pl.BlockSpec((tok, HEAD), lambda h, j, s: (0, h + first_query)) for _ in queries]
            + whole
            + [
                pl.BlockSpec((*x.shape[:2], 2 * HEAD), lambda h, j, s: (0, 0, h + first_head)) for x in w
            ],
            out_specs=pl.BlockSpec((size, HEAD), lambda h, j, s: (j, h)),
            scratch_shapes=[
                pltpu.VMEM((plane, HEAD), jnp.bfloat16),
                pltpu.VMEM((features * cols, 2 * HEAD), jnp.bfloat16),
                pltpu.VMEM((total, 2 * HEAD), jnp.bfloat16),
                pltpu.VMEM((size, HEAD), jnp.float32),
                pltpu.VMEM((size, 2 * HEAD), jnp.float32),
                pltpu.VMEM((cols * group, *before[0][0].shape), jnp.bfloat16),
                pltpu.SemaphoreType.DMA((cols * len(layout),)),
            ],
        ),
        compiler_params=pltpu.CompilerParams(
            dimension_semantics=("arbitrary", "arbitrary"), vmem_limit_bytes=VMEM_LIMIT
        ),
        cost_estimate=pl.CostEstimate(
            flops=heads * plane * total * HEAD * 6,
            transcendentals=heads * plane * total,
            bytes_accessed=total * features * cols * 2,
        ),
        name="attention",
    )(place, *queries, *(x for some in own for x in some), *(x for some in before for x in some), *w)


def project_kernel(scalars, *refs, counts, group, planes):
    a_refs, refs = refs[: sum(counts)], refs[sum(counts) :]
    b_refs, refs = refs[: planes + 1], refs[planes + 1 :]
    outs, (b_sc, sems) = refs[:group], refs[group:]
    step = pl.program_id(0)
    near = scalars[len(counts) + 1] == 1

    @pl.when(step == 0)
    def _():
        copies = [pltpu.make_async_copy(b_refs[k], b_sc.at[k], sems.at[k]) for k in range(planes - 1)]
        for copy in copies:
            copy.start()
        for which, source in ((near, b_refs[planes - 1]), (jnp.logical_not(near), b_refs[planes])):

            @pl.when(which)
            def _():
                copy = pltpu.make_async_copy(source, b_sc.at[planes - 1], sems.at[planes - 1])
                copy.start()
                copy.wait()

        for copy in copies:
            copy.wait()

    out, at = None, 0
    for x, count in enumerate(counts):
        heads = [a_refs[at + i][...] for i in range(count)]
        a = heads[0] if count == 1 else jnp.concatenate(heads, axis=1)
        term = jnp.dot(a, b_sc[scalars[x]], preferred_element_type=jnp.float32)
        out = term if out is None else out + term
        at += count
    for m in range(group):

        @pl.when(step == m)
        def _():
            outs[m][...] = out.astype(outs[m].dtype)


def project(scalars, sets, blocks, group):
    pieces = [x for some in sets for x in some]
    planes = len(blocks) - 1
    tok = pieces[0].shape[0] // group
    depth, width = blocks[0].shape
    count = len(sets)
    return pl.pallas_call(
        functools.partial(
            project_kernel, counts=[len(some) for some in sets], group=group, planes=planes
        ),
        out_shape=[jax.ShapeDtypeStruct((tok, width), jnp.bfloat16)] * group,
        grid_spec=pltpu.PrefetchScalarGridSpec(
            num_scalar_prefetch=1,
            grid=(group,),
            in_specs=[
                pl.BlockSpec((tok, x.shape[1]), lambda j, s: (s[count] ^ j, 0)) for x in pieces
            ]
            + [pl.BlockSpec(memory_space=pl.ANY) for _ in blocks],
            out_specs=[pl.BlockSpec((tok, width), lambda j, s: (0, 0))] * group,
            scratch_shapes=[
                pltpu.VMEM((planes, depth, width), jnp.bfloat16),
                pltpu.SemaphoreType.DMA((planes,)),
            ],
        ),
        compiler_params=pltpu.CompilerParams(
            dimension_semantics=("arbitrary",), vmem_limit_bytes=VMEM_LIMIT
        ),
        cost_estimate=pl.CostEstimate(
            flops=2 * tok * group * planes * depth * width,
            transcendentals=0,
            bytes_accessed=planes * depth * width * 2 + tok * group * planes * depth * 2,
        ),
        name="project",
    )(scalars, *pieces, *blocks)


def per_device(latent, w_kv, queries, w_out):
    planes, group, cols = lax.axis_size("grp"), lax.axis_size("mem"), lax.axis_size("col")
    grp, mem, col = lax.axis_index("grp"), lax.axis_index("mem"), lax.axis_index("col")
    per_col = queries.shape[1] // HEAD
    run = w_out.shape[0] // HEAD
    turns = per_col // (group * run)
    place = jnp.stack([grp, mem, col]).astype(jnp.int32)
    shifts = range(group)

    def swap(x, m):
        return lax.ppermute(x, "mem", [(p, p ^ m) for p in range(group)])

    def gather(x):
        return [x] + [swap(x, m) for m in range(1, group)]

    def exchange(xs):
        return [xs[0]] + [swap(xs[m], m) for m in range(1, group)]

    def up(x, k):
        return lax.ppermute(x, "grp", [(z, z + k) for z in range(planes - k)])

    def across(x, s):
        return lax.ppermute(x, "col", [((c + s) % cols, c) for c in range(cols)])

    def plane_swap(x, k, senders=None):
        senders = range(planes) if senders is None else senders
        return lax.ppermute(x, "grp", [(z, z ^ k) for z in senders])

    far_shift, half = planes - 1, planes // 2
    near = [z for z in range(planes) if abs(z - (z ^ far_shift)) == 1]
    far = [z for z in range(planes) if z not in near]
    is_near = functools.reduce(jnp.logical_or, [grp == z for z in near]).astype(jnp.int32)

    def relay(x):
        last = far_shift ^ half
        return plane_swap(x, last, [z ^ last for z in far])

    width = w_out.shape[1] // group
    first_width = -(-width // (2 * HEAD)) * HEAD
    spans = [(0, first_width), (first_width, width - first_width)]

    def by_turn(n):
        return [(m, n, [(t * group * n, n) for t in range(turns)]) for m in shifts]

    takes = [
        by_turn(run * 2 * HEAD),
        [(m, width, [span]) for span in spans for m in shifts],
        [(m, run * HEAD, [(t * group * run * HEAD, run * HEAD)]) for t in range(turns) for m in shifts],
    ]
    blocks = cut(place, [w_kv, w_out, queries], takes)
    w_mine = exchange(blocks[:group])
    lower = [up(latent, k) for k in range(planes - 1, 0, -1)]
    own = gather(latent)
    w_first = exchange(blocks[group : 2 * group])

    w_mine = jnp.stack(w_mine)
    w_all = [w_mine] + [plane_swap(w_mine, k) for k in range(1, planes)]

    middle_shifts = [half, *(k for k in range(1, far_shift) if k != half)]

    def spread(x):
        x = jnp.concatenate(x)
        return [x] + [plane_swap(x, k) for k in middle_shifts] + [plane_swap(x, far_shift, near)]

    out_first = spread(w_first)
    below = jnp.concatenate(lower)
    count = below.shape[0]
    if group == 4:
        cut_at = count // 32 * 16
        ones, twos = swap(below, 1), swap(below, 2)
        below = [below, ones, twos]
        below += [swap(ones[:cut_at], 2), swap(twos[cut_at:], 1)]
        layout = [(0, 0, count), (1, 0, count), (2, 0, count), (3, 0, cut_at), (3, cut_at, count - cut_at)]
    else:
        below = gather(below)
        layout = [(m, 0, count) for m in shifts]
    my_queries = [exchange(blocks[(3 + t) * group : (4 + t) * group]) for t in range(turns)]
    w_second = exchange(blocks[2 * group : 3 * group])

    owns = [own] + [[across(x, s) for x in own] for s in range(1, cols)]
    belows = [below] + [[across(x, s) for x in below] for s in range(1, cols)]

    calls = [(t, t * run, run) for t in range(turns - 1)]
    calls += [((turns - 1), (turns - 1) * run + i, 1) for i in range(run)]
    results = [[] for _ in range(turns)]
    done = []
    for turn, first_head, heads in calls:
        i = len(done)
        done.append(attention(place, my_queries[turn], owns, belows, layout, w_all, first_head - turn * run, first_head, heads))
        results[turn].append(gather(done[-1]))
        if i == 0:
            w_second, _ = lax.optimization_barrier((w_second, done[0]))
            out_second = spread(w_second)
    middle, _ = lax.optimization_barrier((out_first[1], done[0]))
    first_far = relay(middle)
    middle, _ = lax.optimization_barrier((out_second[1], done[-1]))
    second_far = relay(middle)

    sets, meets = [], []
    for turn in range(turns):
        for s in range(cols):
            some = [[x if s == 0 else across(x, s) for x in part] for part in results[turn]]
            sets.append([part[m] for m in shifts for part in some])
            meets.append((((col + s) % cols) * turns + turn) ^ grp)
    scalars = jnp.stack([*meets, mem, is_near]).astype(jnp.int32)

    def in_order(out, last):
        by_shift = {0: out[0], half: out[1], far_shift: out[-1]}
        by_shift.update(zip(middle_shifts[1:], out[2:-1]))
        return [by_shift[k] for k in range(planes)] + [last]

    mixed = []
    for out, last in ((out_first, first_far), (out_second, second_far)):
        columns = project(scalars, sets, in_order(out, last), group)
        got = exchange(columns)
        stack = jnp.stack(got)
        mixed.append([lax.dynamic_index_in_dim(stack, mem ^ p, 0, False) for p in shifts])
    return jnp.concatenate([part[p] for p in shifts for part in mixed], axis=1)


def solution(mesh):
    rows, cols = mesh.devices.shape
    group = 4
    fine = Mesh(mesh.devices.reshape(rows // group, group, cols), ("grp", "mem", "col"))
    spec = P(("grp", "mem"), "col")

    return jax.shard_map(per_device, mesh=fine, in_specs=(spec,) * 4, out_specs=spec, check_vma=False)
```

```python
import functools
import math

import jax
import jax.numpy as jnp
from jax import lax
from jax.experimental import pallas as pl
from jax.experimental.pallas import tpu as pltpu
from jax.sharding import Mesh, PartitionSpec as P


HEAD = 128
NEG_FILL = -1e30
VMEM_LIMIT = 56 * 1024 * 1024


def cut_kernel(place, *refs, takes):
    ins, outs = refs[: len(takes)], refs[len(takes) :]
    mem = place[1]
    at = 0
    for ref, take in zip(ins, takes):
        for m, stride, parts in take:
            done = 0
            for offset, width in parts:
                first = pl.multiple_of((mem ^ m) * stride + offset, HEAD)
                outs[at][:, done : done + width] = ref[:, pl.ds(first, width)]
                done += width
            at += 1


def cut(place, arrays, takes):
    flat = [(x, take) for x, some in zip(arrays, takes) for take in some]
    widths = [n for _, (_, stride, parts) in flat for n in (stride, *(v for p in parts for v in p))]
    if any(n % HEAD for n in widths):
        mem = place[1]
        return [
            jnp.concatenate(
                [lax.dynamic_slice_in_dim(x, (mem ^ m) * stride + o, n, 1) for o, n in parts], axis=1
            )
            for x, (m, stride, parts) in flat
        ]
    return pl.pallas_call(
        functools.partial(cut_kernel, takes=takes),
        out_shape=[
            jax.ShapeDtypeStruct((x.shape[0], sum(n for _, n in parts)), x.dtype)
            for x, (_, _, parts) in flat
        ],
        grid_spec=pltpu.PrefetchScalarGridSpec(
            num_scalar_prefetch=1,
            grid=(1,),
            in_specs=[pl.BlockSpec(x.shape, lambda i, s: (0, 0)) for x in arrays],
            out_specs=[
                pl.BlockSpec((x.shape[0], sum(n for _, n in parts)), lambda i, s: (0, 0))
                for x, (_, _, parts) in flat
            ],
        ),
        compiler_params=pltpu.CompilerParams(vmem_limit_bytes=VMEM_LIMIT),
        cost_estimate=pl.CostEstimate(
            flops=0, transcendentals=0, bytes_accessed=2 * sum(2 * x.size for x in arrays)
        ),
        name="cut",
    )(place, *arrays)


def attention_kernel(place, *refs, planes, group, cols, layout, rate, parts):
    q_refs, refs = refs[:group], refs[group:]
    own, refs = refs[: cols * group], refs[cols * group :]
    before, refs = refs[: cols * len(layout)], refs[cols * len(layout) :]
    w_refs, refs = refs[:planes], refs[planes:]
    o_ref, q_sc, w_sc, kv_sc, m_sc, acc_sc, before_sc, sems = refs
    grp, mem, col = place[0], place[1], place[2]
    tok, features = own[0].shape
    plane = tok * group
    earlier = (planes - 1) * plane
    block = pl.program_id(1)
    size = o_ref.shape[0]
    rows = size // parts
    depth = w_refs[0].shape[1]

    first_step = jnp.logical_and(pl.program_id(0) == 0, block == 0)
    copies = []
    for s in range(cols):
        for i, (m, start, count) in enumerate(layout):
            at = s * len(layout) + i
            target = before_sc.at[s * group + m, pl.ds(start, count), :]
            copies.append(pltpu.make_async_copy(before[at], target, sems.at[at]))

    @pl.when(first_step)
    def _():
        for copy in copies:
            copy.start()

    def expand(load, to):
        out = None
        for s in range(cols):
            w = w_sc[pl.ds(pl.multiple_of(((col + s) % cols) * features, features), features), :]
            term = jnp.dot(load(s), w, preferred_element_type=jnp.float32)
            out = term if out is None else out + term
        kv_sc[to, :] = out.astype(kv_sc.dtype)

    @pl.when(block == 0)
    def _():
        for m in range(group):
            q_sc[pl.ds(pl.multiple_of((mem ^ m) * tok, tok), tok), :] = q_refs[m][...]
            for k in range(planes):
                first = ((grp ^ k) * group + (mem ^ m)) * depth
                w_sc[pl.ds(pl.multiple_of(first, depth), depth), :] = w_refs[k][m]
        for m in range(group):
            first = earlier + (mem ^ m) * tok
            expand(lambda s: own[s * group + m][...], pl.ds(pl.multiple_of(first, tok), tok))

    m_sc[...] = jnp.full_like(m_sc, NEG_FILL)
    acc_sc[...] = jnp.zeros_like(acc_sc)
    base = pl.multiple_of(block * size, size)

    def step(first, width, query_at=None):
        keys = kv_sc[pl.ds(first, width), :HEAD]
        values = kv_sc[pl.ds(first, width), HEAD:]
        values = jnp.concatenate([values, jnp.ones_like(values)], axis=1)
        scores = []
        for u in range(parts):
            s = lax.dot_general(
                q_sc[pl.ds(base + u * rows, rows), :],
                keys,
                (((1,), (1,)), ((), ())),
                preferred_element_type=jnp.float32,
            )
            if query_at is not None:
                row = lax.broadcasted_iota(jnp.int32, s.shape, 0) + (query_at + u * rows)
                column = lax.broadcasted_iota(jnp.int32, s.shape, 1)
                s = jnp.where(column <= row, s, NEG_FILL)
            scores.append(s)
        for u in range(parts):
            at = slice(u * rows, (u + 1) * rows)
            old = m_sc[at]
            new = jnp.maximum(old, jnp.max(scores[u], axis=1, keepdims=True))
            m_sc[at] = new
            shifted = scores[u] - jnp.tile(new, (1, width // HEAD))
            weights = jnp.exp2(shifted * rate).astype(jnp.bfloat16)
            again = jnp.exp2((old - new) * rate)
            acc_sc[at] = acc_sc[at] * jnp.concatenate([again, again], axis=1) + jnp.dot(
                weights, values, preferred_element_type=jnp.float32
            )

    def plane_step(t, _):
        step(pl.multiple_of(t * plane, plane), plane)
        return 0

    for b in range(plane // size):

        @pl.when(block == b)
        def _():
            step(earlier, (b + 1) * size, b * size)

    @pl.when(first_step)
    def _():
        for copy in copies:
            copy.wait()

    @pl.when(block == 0)
    def _():
        def plane_before(t, _):
            at = pl.ds(pl.multiple_of(t * tok, tok), tok)
            for m in range(group):
                expand(
                    lambda s: before_sc[s * group + m, at, :],
                    pl.ds(pl.multiple_of(t * plane + m * tok, tok), tok),
                )
            return 0

        lax.fori_loop(planes - 1 - grp, planes - 1, plane_before, 0)

    lax.fori_loop(planes - 1 - grp, planes - 1, plane_step, 0)
    o_ref[...] = (acc_sc[:, :HEAD] / acc_sc[:, HEAD:]).astype(o_ref.dtype)


def attention(place, queries, own, before, layout, w, first_query, first_head, heads):
    planes, group, cols = len(w), len(queries), len(own)
    tok, features = own[0][0].shape
    plane = tok * group
    total = planes * plane
    size = plane
    fixed = lambda h, j, s: (0, 0)
    whole = [pl.BlockSpec(x.shape, fixed, pipeline_mode=pl.Buffered(1)) for x in own[0] * cols]
    whole += [pl.BlockSpec(memory_space=pl.ANY) for _ in before[0] * cols]
    return pl.pallas_call(
        functools.partial(
            attention_kernel,
            planes=planes,
            group=group,
            cols=cols,
            layout=layout,
            rate=HEAD**-0.5 * math.log2(math.e),
            parts=2,
        ),
        out_shape=jax.ShapeDtypeStruct((plane, heads * HEAD), jnp.bfloat16),
        grid_spec=pltpu.PrefetchScalarGridSpec(
            num_scalar_prefetch=1,
            grid=(heads, plane // size),
            in_specs=[pl.BlockSpec((tok, HEAD), lambda h, j, s: (0, h + first_query)) for _ in queries]
            + whole
            + [
                pl.BlockSpec((*x.shape[:2], 2 * HEAD), lambda h, j, s: (0, 0, h + first_head)) for x in w
            ],
            out_specs=pl.BlockSpec((size, HEAD), lambda h, j, s: (j, h)),
            scratch_shapes=[
                pltpu.VMEM((plane, HEAD), jnp.bfloat16),
                pltpu.VMEM((features * cols, 2 * HEAD), jnp.bfloat16),
                pltpu.VMEM((total, 2 * HEAD), jnp.bfloat16),
                pltpu.VMEM((size, HEAD), jnp.float32),
                pltpu.VMEM((size, 2 * HEAD), jnp.float32),
                pltpu.VMEM((cols * group, *before[0][0].shape), jnp.bfloat16),
                pltpu.SemaphoreType.DMA((cols * len(layout),)),
            ],
        ),
        compiler_params=pltpu.CompilerParams(
            dimension_semantics=("arbitrary", "arbitrary"), vmem_limit_bytes=VMEM_LIMIT
        ),
        cost_estimate=pl.CostEstimate(
            flops=heads * plane * total * HEAD * 6,
            transcendentals=heads * plane * total,
            bytes_accessed=total * features * cols * 2,
        ),
        name="attention",
    )(place, *queries, *(x for some in own for x in some), *(x for some in before for x in some), *w)


def project_kernel(scalars, *refs, counts, group, planes, carried, last):
    a_refs, refs = refs[: sum(counts)], refs[sum(counts) :]
    b_refs, refs = refs[: planes + 1], refs[planes + 1 :]
    if carried:
        part_ref, refs = refs[0], refs[1:]
    outs, (b_sc, sems) = refs[:-2], refs[-2:]
    step = pl.program_id(0)
    near = scalars[len(counts) + 1] == 1

    for x in range(len(counts)):
        for k in range(planes + 1):
            slot = min(k, planes - 1)
            wanted = jnp.logical_and(step == 0, scalars[x] == slot)
            if k >= planes - 1:
                wanted = jnp.logical_and(wanted, near if k == planes - 1 else jnp.logical_not(near))

            @pl.when(wanted)
            def _():
                pltpu.make_async_copy(b_refs[k], b_sc.at[x], sems.at[x]).start()

    @pl.when(step == 0)
    def _():
        for x in range(len(counts)):
            pltpu.make_async_copy(b_refs[0], b_sc.at[x], sems.at[x]).wait()

    out, at = part_ref[...] if carried else None, 0
    for x, count in enumerate(counts):
        heads = [a_refs[at + i][...] for i in range(count)]
        a = heads[0] if count == 1 else jnp.concatenate(heads, axis=1)
        term = jnp.dot(a, b_sc[x], preferred_element_type=jnp.float32)
        out = term if out is None else out + term
        at += count
    if last:
        for m in range(group):

            @pl.when(step == m)
            def _():
                outs[m][...] = out.astype(outs[m].dtype)
    else:
        outs[0][...] = out


def project(meets, mem, is_near, sets, blocks, group, carried=None, last=True):
    scalars = jnp.stack([*meets, mem, is_near]).astype(jnp.int32)
    pieces = [x for some in sets for x in some]
    planes = len(blocks) - 1
    rows = pieces[0].shape[0]
    tok = rows // group
    depth, width = blocks[0].shape
    count = len(sets)
    part_spec = pl.BlockSpec((tok, width), lambda j, s: (j, 0))
    parts = [] if carried is None else [carried]
    out = pl.pallas_call(
        functools.partial(
            project_kernel,
            counts=[len(some) for some in sets],
            group=group,
            planes=planes,
            carried=carried is not None,
            last=last,
        ),
        out_shape=[jax.ShapeDtypeStruct((tok, width), jnp.bfloat16)] * group
        if last
        else [jax.ShapeDtypeStruct((rows, width), jnp.float32)],
        grid_spec=pltpu.PrefetchScalarGridSpec(
            num_scalar_prefetch=1,
            grid=(group,),
            in_specs=[
                pl.BlockSpec((tok, x.shape[1]), lambda j, s: (s[count] ^ j, 0)) for x in pieces
            ]
            + [pl.BlockSpec(memory_space=pl.ANY) for _ in blocks]
            + [part_spec for _ in parts],
            out_specs=[pl.BlockSpec((tok, width), lambda j, s: (0, 0))] * group if last else [part_spec],
            scratch_shapes=[
                pltpu.VMEM((count, depth, width), jnp.bfloat16),
                pltpu.SemaphoreType.DMA((count,)),
            ],
        ),
        compiler_params=pltpu.CompilerParams(
            dimension_semantics=("arbitrary",), vmem_limit_bytes=VMEM_LIMIT
        ),
        cost_estimate=pl.CostEstimate(
            flops=2 * rows * count * depth * width,
            transcendentals=0,
            bytes_accessed=count * depth * width * 2 + rows * count * depth * 2,
        ),
        name="project",
    )(scalars, *pieces, *blocks, *parts)
    return out if last else out[0]


def per_device(latent, w_kv, queries, w_out):
    planes, group, cols = lax.axis_size("grp"), lax.axis_size("mem"), lax.axis_size("col")
    grp, mem, col = lax.axis_index("grp"), lax.axis_index("mem"), lax.axis_index("col")
    per_col = queries.shape[1] // HEAD
    run = w_out.shape[0] // HEAD
    turns = per_col // (group * run)
    place = jnp.stack([grp, mem, col]).astype(jnp.int32)
    shifts = range(group)

    def swap(x, m):
        return lax.ppermute(x, "mem", [(p, p ^ m) for p in range(group)])

    def gather(x):
        return [x] + [swap(x, m) for m in range(1, group)]

    def exchange(xs):
        return [xs[0]] + [swap(xs[m], m) for m in range(1, group)]

    def up(x, k):
        return lax.ppermute(x, "grp", [(z, z + k) for z in range(planes - k)])

    def across(x, s):
        return lax.ppermute(x, "col", [((c + s) % cols, c) for c in range(cols)])

    def plane_swap(x, k, senders=None):
        senders = range(planes) if senders is None else senders
        return lax.ppermute(x, "grp", [(z, z ^ k) for z in senders])

    far_shift, half = planes - 1, planes // 2
    near = [z for z in range(planes) if abs(z - (z ^ far_shift)) == 1]
    far = [z for z in range(planes) if z not in near]
    is_near = functools.reduce(jnp.logical_or, [grp == z for z in near]).astype(jnp.int32)

    def relay(x):
        last = far_shift ^ half
        return plane_swap(x, last, [z ^ last for z in far])

    width = w_out.shape[1] // group
    first_width = -(-width // (2 * HEAD)) * HEAD
    spans = [(0, first_width), (first_width, width - first_width)]

    def by_turn(n):
        return [(m, n, [(t * group * n, n) for t in range(turns)]) for m in shifts]

    takes = [
        by_turn(run * 2 * HEAD),
        [(m, width, [span]) for span in spans for m in shifts],
        [(m, run * HEAD, [(t * group * run * HEAD, run * HEAD)]) for t in range(turns) for m in shifts],
    ]
    blocks = cut(place, [w_kv, w_out, queries], takes)
    w_mine = exchange(blocks[:group])
    lower = [up(latent, k) for k in range(planes - 1, 0, -1)]
    own = gather(latent)
    w_first = exchange(blocks[group : 2 * group])

    w_mine = jnp.stack(w_mine)
    w_all = [w_mine] + [plane_swap(w_mine, k) for k in range(1, planes)]

    middle_shifts = [half, *(k for k in range(1, far_shift) if k != half)]

    def spread(x):
        x = jnp.concatenate(x)
        return [x] + [plane_swap(x, k) for k in middle_shifts] + [plane_swap(x, far_shift, near)]

    out_first = spread(w_first)
    below = jnp.concatenate(lower)
    count = below.shape[0]
    if group == 4:
        cut_at = count // 32 * 16
        ones, twos = swap(below, 1), swap(below, 2)
        below = [below, ones, twos]
        below += [swap(ones[:cut_at], 2), swap(twos[cut_at:], 1)]
        layout = [(0, 0, count), (1, 0, count), (2, 0, count), (3, 0, cut_at), (3, cut_at, count - cut_at)]
    else:
        below = gather(below)
        layout = [(m, 0, count) for m in shifts]
    my_queries = [exchange(blocks[(3 + t) * group : (4 + t) * group]) for t in range(turns)]
    w_second = exchange(blocks[2 * group : 3 * group])

    owns = [own] + [[across(x, s) for x in own] for s in range(1, cols)]
    belows = [below] + [[across(x, s) for x in below] for s in range(1, cols)]

    calls = [(t, t * run, run) for t in range(turns - 1)]
    calls += [((turns - 1), (turns - 1) * run + i, 1) for i in range(run)]
    results = [[] for _ in range(turns)]
    done = []
    for turn, first_head, heads in calls:
        i = len(done)
        done.append(attention(place, my_queries[turn], owns, belows, layout, w_all, first_head - turn * run, first_head, heads))
        results[turn].append(gather(done[-1]))
        if i == 0:
            w_second, _ = lax.optimization_barrier((w_second, done[0]))
            out_second = spread(w_second)
    middle, _ = lax.optimization_barrier((out_first[1], done[0]))
    first_far = relay(middle)
    middle, _ = lax.optimization_barrier((out_second[1], done[-1]))
    second_far = relay(middle)

    sets, meets = [], []
    for turn in range(turns):
        for s in range(cols):
            some = [[x if s == 0 else across(x, s) for x in part] for part in results[turn]]
            sets.append([part[m] for m in shifts for part in some])
            meets.append((((col + s) % cols) * turns + turn) ^ grp)

    def in_order(out, last):
        by_shift = {0: out[0], half: out[1], far_shift: out[-1]}
        by_shift.update(zip(middle_shifts[1:], out[2:-1]))
        return [by_shift[k] for k in range(planes)] + [last]

    mixed = []
    for out, last in ((out_first, first_far), (out_second, second_far)):
        rows, part, early = in_order(out, last), None, 0
        if not mixed and turns > 1:
            early = cols * (turns - 1)
            part = project(meets[:early], mem, is_near, sets[:early], rows, group, None, False)
        columns = project(meets[early:], mem, is_near, sets[early:], rows, group, part)
        got = exchange(columns)
        stack = jnp.stack(got)
        mixed.append([lax.dynamic_index_in_dim(stack, mem ^ p, 0, False) for p in shifts])
    return jnp.concatenate([part[p] for p in shifts for part in mixed], axis=1)


def solution(mesh):
    rows, cols = mesh.devices.shape
    group = 4
    fine = Mesh(mesh.devices.reshape(rows // group, group, cols), ("grp", "mem", "col"))
    spec = P(("grp", "mem"), "col")

    return jax.shard_map(per_device, mesh=fine, in_specs=(spec,) * 4, out_specs=spec, check_vma=False)
```
